512 devices in a mesh: feeder: 8 (over z_hi, y), tm: 64 (over z_lo, x, core).
Axes of the slice: x: 4, y: 4, z: 16 (z_hi: 2, z_lo: 8; z = z_hi * 8 + z_lo), core: 2. Of those that a mesh axis runs over, the one named last changes fastest.
Arguments:
- observed: bfloat16 [24576, 32768], P('feeder', 'tm'), may hold values from -16 to 16
- mask_words: int32 [24576, 4096], P('feeder', 'tm'), may hold values from 0 to 255, as said below
- feeder_factor: float32 [24576, 64], P('feeder'), may hold values from -6 to 6
- time_factor: float32 [64, 32768], P(None, 'tm'), may hold values from -0.75 to 0.75
- ar_weight: float32 [10, 64], replicated, may hold values from -0.5 to 0.5
- lags: int32 [10], replicated, may hold values from 1 to 1440, as said below
- moment_first: float32 [24576, 64], P(('feeder', 'tm')), may hold values from -0.6 to 0.6
- moment_second: float32 [24576, 64], P(('feeder', 'tm')), may hold values from 0.01 to 1
Outputs:
- new_factor: float32 [24576, 64], P(('feeder', 'tm'))
- new_first: float32 [24576, 64], P(('feeder', 'tm'))
- new_second: float32 [24576, 64], P(('feeder', 'tm'))
- time_grad: float32 [64, 32768], P('feeder', 'tm')
The draws below stay inside these ranges and needn't reach their ends.
Inputs may be any that keep to these rules, and one draw needn't show every extreme that they name: `mask_words`: bit b of word w of a feeder's row tells whether minute 8 w + b is observed (1) or not (0). Eight lags of 1 to 12, one lag between 30 and 90, and one lag of exactly 1440; lags may repeat.
All inputs are finite; a program needn't handle non-finite values.
Results may differ from the reference program's by a relative error of at most 0.00065.
Values sent between devices are 32-bit elements; how exact they have to be, the bound alone decides.
No kernel may reach another device: no remote copies, remote signals or barrier semaphores. Data moves between devices by JAX's collectives and lax.ppermute only.
A program may use at most 64 MiB of HBM per device.

```python
import math
import jax
import jax.numpy as jnp
from jax import lax

K = 64
NLAG = 10
LAGMAX = 1440
NF = 3072
N = 24576
T_SIZE = 32768
WORDS = 4096
N_FEEDER = 8


def draw_mask_words(key, part):
    base_key = jax.random.fold_in(key, 5)
    place_key = jax.random.fold_in(key, 7)
    words = jax.random.randint(base_key, (N, WORDS), 0, 256, dtype=jnp.int32)
    row_pick = jax.random.randint(place_key, (), 0, N, dtype=jnp.int32)
    word_pick = jax.random.randint(jax.random.fold_in(place_key, 1), (), 0, WORDS, dtype=jnp.int32)
    words = words.at[row_pick, word_pick].set(jnp.int32(0))
    words = words.at[(row_pick + 1) % N, word_pick].set(jnp.int32(255))
    return words


def draw_lags(key, part):
    first_key = jax.random.fold_in(key, 11)
    second_key = jax.random.fold_in(key, 23)
    short_lags = jax.random.permutation(first_key, 12)[:8].astype(jnp.int32) + 1
    middle = jax.random.randint(second_key, (1,), max(LAGMAX // 48, 1), LAGMAX // 16 + 1, dtype=jnp.int32)
    longest = jnp.full((1,), LAGMAX, dtype=jnp.int32)
    return jnp.concatenate([short_lags, middle, longest]).astype(jnp.int32)


def with_spikes(array, rng, source, target, parts, factor):
    owner, partner = [(jnp.arange(array.shape[axis_at]) // (array.shape[axis_at] // parts)).reshape([-1 if axis == axis_at else 1 for axis in range(array.ndim)]) for axis_at in (source, target)]
    chosen = jax.random.permutation(rng, parts)[partner]
    strong = (owner == chosen) | (owner == (partner + parts // 2) % parts)
    return jnp.where(strong, factor * array, array)


def shard_levels(rng, shape, split, smallest, high):
    loudness = 1.0
    for dim, parts in split:
        steps = jax.random.uniform(jax.random.fold_in(jax.random.fold_in(rng, 6), dim), (parts,), jnp.float32, smallest / len(split), high / len(split))
        loudness = loudness * jnp.repeat(jnp.exp(steps), shape[dim] // parts).reshape((-1,) + (1,) * (len(shape) - 1 - dim))
    return loudness


def noise(key, dims, spread, most, shards=(), held_as=jnp.bfloat16):
    gain = shard_levels(key, dims, shards, -0.22, 0.18) if shards else 1.0
    array = jax.random.normal(key, dims, jnp.float32) * spread * gain
    return jnp.minimum(jnp.maximum(array, -most), most).astype(held_as)


def noise_with(own_key, shape, scale, reach, shards, heavy, held_as=jnp.bfloat16):
    drawn = scale * jax.random.normal(own_key, shape, jnp.float32)
    if shards:
        drawn = drawn * shard_levels(own_key, shape, shards, -0.22, 0.18)
    return jnp.clip(with_spikes(drawn, jax.random.fold_in(own_key, 3), *heavy), -reach, reach).astype(held_as)


def setup_inputs(seed: int = 0) -> dict:
    key_of = jax.random.split(jax.random.key(seed), 9)
    observed = noise_with(key_of[0], (N, T_SIZE), 1.0, 16.0, ((0, 8), (1, 64)), (1, 0, 64, 4.0))
    mask_words = draw_mask_words(jax.random.fold_in(key_of[8], 71), 0)
    feeder_factor = noise(key_of[2], (N, K), 1.0, 6.0, ((0, 8),), jnp.float32)
    time_factor = noise(key_of[3], (K, T_SIZE), 0.125, 0.75, ((1, 64),), jnp.float32)
    ar_weight = jnp.clip(jax.random.uniform(key_of[4], (NLAG, K), jnp.float32, -0.5, 0.5), -0.5, 0.5)
    lags = draw_lags(jax.random.fold_in(key_of[8], 71), 0)
    moment_first = noise(key_of[6], (N, K), 0.1, 0.6, ((0, 512),), jnp.float32)
    moment_second = jnp.clip(jnp.exp(math.log(1.0) - 4.6051702 * jax.random.uniform(key_of[7], (N, K), jnp.float32) ** shard_levels(key_of[7], (N, K), ((0, 512),), -0.2, 0.2)), 0.01, 1.0)
    return {"observed": observed, "mask_words": mask_words, "feeder_factor": feeder_factor, "time_factor": time_factor, "ar_weight": ar_weight, "lags": lags, "moment_first": moment_first, "moment_second": moment_second}


DATA_WEIGHT = 1.0 / 64.0
LAM_F = 0.1
LAM_X = 0.01
LAM_AR = 8.0
BETA_ONE = 0.9
BETA_TWO = 0.999
BIAS_FIRST = 1.0 - 0.9 ** 8
BIAS_SECOND = 1.0 - 0.999 ** 8
LEARNING_RATE = 0.05
ADAM_EPS = 1e-08

def unpack_mask(words):
    shifts = jnp.arange(8, dtype=jnp.int32)
    bits = words[:, :, None] >> shifts & 1
    return bits.reshape(words.shape[0], words.shape[1] * 8).astype(jnp.float32)

def reference(observed, mask_words, feeder_factor, time_factor, ar_weight, lags, moment_first, moment_second):
    time_half = time_factor.astype(jnp.bfloat16)
    obs_blocks = observed.reshape(N_FEEDER, NF, T_SIZE)
    word_blocks = mask_words.reshape(N_FEEDER, NF, WORDS)
    factor_blocks = feeder_factor.reshape(N_FEEDER, NF, K)

    def block_terms(carry, pieces):
        obs_block, word_block, factor_block = pieces
        factor_half = factor_block.astype(jnp.bfloat16)
        predicted = jnp.dot(factor_half, time_half, preferred_element_type=jnp.float32)
        residual = (unpack_mask(word_block) * (predicted - obs_block.astype(jnp.float32))).astype(jnp.bfloat16)
        grad_rows = jnp.dot(residual, time_half.T, preferred_element_type=jnp.float32)
        time_term = lax.dot_general(factor_half, residual, (((0,), (0,)), ((), ())), preferred_element_type=jnp.float32)
        return (carry + time_term, grad_rows)
    time_data, grad_blocks = lax.scan(block_terms, jnp.zeros((K, T_SIZE), jnp.float32), (obs_blocks, word_blocks, factor_blocks))
    factor_grad = DATA_WEIGHT * grad_blocks.reshape(N, K) + LAM_F * feeder_factor
    padded = jnp.concatenate([jnp.zeros((K, LAGMAX), jnp.float32), time_factor], axis=1)
    predicted_ar = jnp.zeros((K, T_SIZE), jnp.float32)
    for index in range(NLAG):
        start = (LAGMAX - lags[index]).astype(jnp.int32)
        predicted_ar = predicted_ar + ar_weight[index][:, None] * lax.dynamic_slice_in_dim(padded, start, T_SIZE, 1)
    columns = jnp.arange(T_SIZE, dtype=jnp.int32)
    errors = jnp.where(columns[None, :] >= LAGMAX, time_factor - predicted_ar, 0.0)
    ahead = jnp.concatenate([errors, jnp.zeros((K, LAGMAX), jnp.float32)], axis=1)
    carried = jnp.zeros((K, T_SIZE), jnp.float32)
    for index in range(NLAG):
        start = lags[index].astype(jnp.int32)
        carried = carried + ar_weight[index][:, None] * lax.dynamic_slice_in_dim(ahead, start, T_SIZE, 1)
    adjoint = errors - carried
    time_grad = DATA_WEIGHT * time_data + LAM_AR * adjoint + LAM_X * time_factor
    new_first = BETA_ONE * moment_first + (1.0 - BETA_ONE) * factor_grad
    new_second = BETA_TWO * moment_second + (1.0 - BETA_TWO) * factor_grad * factor_grad
    update = LEARNING_RATE * (new_first / BIAS_FIRST) / (jnp.sqrt(new_second / BIAS_SECOND) + ADAM_EPS)
    new_factor = feeder_factor - update
    return (new_factor, new_first, new_second, time_grad)
```

```python
import functools

import jax
import jax.numpy as jnp
from jax import lax
from jax.experimental import pallas as pl
from jax.experimental.pallas import tpu as pltpu
from jax.sharding import Mesh
from jax.sharding import PartitionSpec as P

LAGMAX = 1440
DATA_WEIGHT = 1.0 / 64.0
LAM_F = 0.1
LAM_X = 0.01
LAM_AR = 8.0
BETA_ONE = 0.9
BETA_TWO = 0.999
BIAS_FIRST = 1.0 - 0.9**8
BIAS_SECOND = 1.0 - 0.999**8
LEARNING_RATE = 0.05
ADAM_EPS = 1e-08

AXES = ("z_hi", "y", "z_lo", "x", "core")
FEEDER_AXES, TM_AXES, PLANE_AXES = AXES[:2], AXES[2:], AXES[3:]
PLANES, PLANE = 8, 8
TM = PLANES * PLANE
FEEDER = 8
SHARE = 48
BAND = 8
SPAN = 512
TILES = SPAN // 128
MAIN_ROWS = PLANES * SHARE // 2
ROWS = MAIN_ROWS + BAND * TILES
HOPS = 3
CHUNKS = (HOPS + 1) * TILES


def main_kernel(
    place, observed, words, factor, time, spread, shares, time_out, total, *, steps, planes
):
    step = pl.program_id(0)
    factor_half = factor[...].astype(jnp.bfloat16)
    time_half = time[...].astype(jnp.bfloat16)
    predicted = lax.dot_general(
        factor_half, time_half, (((0,), (0,)), ((), ())), preferred_element_type=jnp.float32
    )
    wide = lax.dot_general(
        words[...].astype(jnp.float32).astype(jnp.bfloat16),
        spread[...],
        (((0,), (0,)), ((), ())),
        preferred_element_type=jnp.float32,
    ).astype(jnp.int32)
    bit = jnp.left_shift(1, lax.broadcasted_iota(jnp.int32, wide.shape, 1) & 7)
    residual = jnp.where(
        (wide & bit) != 0, predicted - observed[...].astype(jnp.float32), 0.0
    ).astype(jnp.bfloat16)
    rows = DATA_WEIGHT * lax.dot_general(
        residual, time_half, (((1,), (1,)), ((), ())), preferred_element_type=jnp.float32
    )
    half = SHARE // 2
    for plane in range(planes):
        for local in range(PLANE):
            start = (plane * PLANE + local) * SHARE
            packed = jnp.concatenate(
                [rows[start : start + half], rows[start + half : start + SHARE]], axis=1
            )
            shares[local, pl.ds(pl.multiple_of((step * planes + plane) * half, 8), half)] = packed
    term = jnp.dot(factor_half, residual, preferred_element_type=jnp.float32)

    @pl.when(step == 0)
    def _():
        total[...] = term
        own = time[pl.ds(pl.multiple_of(place[0] * BAND, BAND), BAND), :]
        for tile in range(TILES):
            at = MAIN_ROWS + BAND * tile
            for local in range(PLANE):
                shares[local, at : at + BAND] = own[:, 128 * tile : 128 * tile + 128]

    @pl.when(step > 0)
    def _():
        total[...] = total[...] + term

    @pl.when(step == steps - 1)
    def _():
        for band in range(FEEDER):
            z, y = band >> 2, band & 3
            time_out[y, place[1] ^ z] = DATA_WEIGHT * total[BAND * band : BAND * band + BAND]


def main_terms(observed, words, factor, time, place, steps=4):
    feeders, span = observed.shape
    ranks, block = factor.shape[0], feeders // steps
    spread = (
        lax.broadcasted_iota(jnp.int32, (words.shape[0], span), 1) // 8
        == lax.broadcasted_iota(jnp.int32, (words.shape[0], span), 0)
    ).astype(jnp.bfloat16)
    return pl.pallas_call(
        functools.partial(main_kernel, steps=steps, planes=PLANES // steps),
        grid_spec=pltpu.PrefetchScalarGridSpec(
            num_scalar_prefetch=1,
            grid=(steps,),
            in_specs=[
                pl.BlockSpec((block, span), lambda s, place: (s, 0)),
                pl.BlockSpec((words.shape[0], block), lambda s, place: (0, s)),
                pl.BlockSpec((ranks, block), lambda s, place: (0, s)),
                pl.BlockSpec((ranks, span), lambda s, place: (0, 0)),
                pl.BlockSpec((words.shape[0], span), lambda s, place: (0, 0)),
            ],
            out_specs=[
                pl.BlockSpec((PLANE, ROWS, 128), lambda s, place: (0, 0, 0)),
                pl.BlockSpec((4, 2, BAND, span), lambda s, place: (0, 0, 0, 0)),
            ],
            scratch_shapes=[pltpu.VMEM((ranks, span), jnp.float32)],
        ),
        out_shape=[
            jax.ShapeDtypeStruct((PLANE, ROWS, 128), jnp.float32),
            jax.ShapeDtypeStruct((4, 2, BAND, span), jnp.float32),
        ],
        cost_estimate=pl.CostEstimate(flops=805306368, bytes_accessed=6_000_000, transcendentals=0),
        name="main_terms",
    )(place, observed, words, factor, time, spread)


def shifted_tiles(tiles, start, count, read):
    first, lane = start >> 7, start & 127
    back = (128 - lane) & 127
    rolled = [pltpu.roll(read(first + i), back, 1) for i in range(count + 1)]
    inside = lax.broadcasted_iota(jnp.int32, (BAND, 128), 1) < 128 - lane
    return [jnp.where(inside, rolled[i], rolled[i + 1]) for i in range(count)]


def ar_kernel(
    place, lags, weights, plane, beside, home, away, time_grad, spans, errors, weight_rows
):
    edge = HOPS * TILES
    for span in range(HOPS):
        for tile in range(TILES):
            value = beside[span, BAND * tile : BAND * tile + BAND]
            spans[span * TILES + tile] = value
            spans[edge + PLANE * TILES + span * TILES + tile] = value
    for span in range(PLANE):
        for tile in range(TILES):
            spans[edge + span * TILES + tile] = plane[span, BAND * tile : BAND * tile + BAND]
    weight_rows[...] = weights[...].T
    mine = weight_rows[pl.ds(pl.multiple_of(place[0] * BAND, BAND), BAND), :]
    own_tile = edge + place[3] * TILES
    own_column = own_tile * 128
    count = lags.shape[0]
    gains = [jnp.broadcast_to(mine[:, k : k + 1], (BAND, 128)) for k in range(count)]
    parts = [jnp.zeros((BAND, 128), jnp.float32) for _ in range(CHUNKS)]
    for k in range(count):
        moved = shifted_tiles(spans, own_column - lags[k], CHUNKS, lambda i: spans[i])
        parts = [part + gains[k] * tile for part, tile in zip(parts, moved)]
    lane = lax.broadcasted_iota(jnp.int32, (BAND, 128), 1)
    first = place[2] * SPAN
    for chunk in range(CHUNKS):
        column = first + 128 * chunk + lane
        inside = (column >= LAGMAX) & (column < TM * SPAN)
        errors[chunk] = jnp.where(inside, spans[own_tile + chunk] - parts[chunk], 0.0)
    errors[CHUNKS] = jnp.zeros((BAND, 128), jnp.float32)
    carried = [jnp.zeros((BAND, 128), jnp.float32) for _ in range(TILES)]
    for k in range(count):
        moved = shifted_tiles(errors, lags[k], TILES, lambda i: errors[i])
        carried = [part + gains[k] * tile for part, tile in zip(carried, moved)]
    for tile in range(TILES):
        at = slice(128 * tile, 128 * tile + 128)
        time_grad[:, at] = (
            home[:, at]
            + away[:, at]
            + LAM_AR * (errors[tile] - carried[tile])
            + LAM_X * spans[own_tile + tile]
        )


def ar_terms(place, lags, weights, plane, beside, home, away):
    in_vmem = pl.BlockSpec(memory_space=pltpu.VMEM)
    in_smem = pl.BlockSpec(memory_space=pltpu.SMEM)
    tiles = (2 * HOPS + PLANE) * TILES
    return pl.pallas_call(
        ar_kernel,
        in_specs=[in_smem, in_smem] + [in_vmem] * 5,
        out_specs=in_vmem,
        out_shape=jax.ShapeDtypeStruct((BAND, SPAN), jnp.float32),
        scratch_shapes=[
            pltpu.VMEM((tiles + 1, BAND, 128), jnp.float32),
            pltpu.VMEM((CHUNKS + 1, BAND, 128), jnp.float32),
            pltpu.VMEM(weights.shape[::-1], jnp.float32),
        ],
        cost_estimate=pl.CostEstimate(flops=2_000_000, bytes_accessed=400_000, transcendentals=0),
        compiler_params=pltpu.CompilerParams(vmem_limit_bytes=8 << 20),
        name="ar_terms",
    )(place, lags, weights, plane, beside, home, away)


def per_device(
    observed, mask_words, feeder_factor, time_factor, ar_weight, lags, moment_first, moment_second
):
    ranks = time_factor.shape[0]
    tm_place = lax.axis_index(TM_AXES)
    plane_place = lax.axis_index(PLANE_AXES)
    place = jnp.stack(
        [lax.axis_index(FEEDER_AXES), lax.axis_index("z_hi"), tm_place, plane_place]
    ).astype(jnp.int32)

    shares, time_part = main_terms(observed, mask_words.T, feeder_factor.T, time_factor, place)
    bands = lax.all_to_all(time_part, "y", 0, 0, tiled=True)
    got = lax.all_to_all(shares, PLANE_AXES, 0, 0, tiled=True)
    bands = bands.sum(0)
    away = lax.ppermute(bands[1], "z_hi", [(0, 1), (1, 0)])

    plane = got[:, MAIN_ROWS:]
    passed = jnp.where(plane_place < PLANE // 2, plane[PLANE - HOPS :], plane[:HOPS])
    pairs = [(t, t + PLANE) for t in range(TM - PLANE) if t % PLANE < PLANE // 2]
    pairs += [(t, t - PLANE) for t in range(PLANE, TM) if t % PLANE >= PLANE // 2]
    beside = lax.ppermute(passed, TM_AXES, pairs)
    planes = got[:, :MAIN_ROWS].sum(0).reshape(PLANES, SHARE // 2, 128)
    share = lax.all_to_all(planes, "z_lo", 0, 0, tiled=True).sum(0)
    time_grad = ar_terms(place, lags, ar_weight, plane, beside, bands[0], away)

    grad_share = jnp.concatenate([share[:, :ranks], share[:, ranks:]], axis=0)
    own_factor = lax.dynamic_slice_in_dim(feeder_factor, tm_place * SHARE, SHARE, 0)
    factor_grad = grad_share + LAM_F * own_factor
    new_first = BETA_ONE * moment_first + (1.0 - BETA_ONE) * factor_grad
    new_second = BETA_TWO * moment_second + (1.0 - BETA_TWO) * factor_grad * factor_grad
    update = (
        LEARNING_RATE * (new_first / BIAS_FIRST) / (jnp.sqrt(new_second / BIAS_SECOND) + ADAM_EPS)
    )
    return (own_factor - update, new_first, new_second, time_grad)


def solution(mesh):
    fine = Mesh(mesh.devices.reshape(2, 4, 8, 4, 2), AXES)
    rows = P(AXES, None)
    placed = (
        P(FEEDER_AXES, TM_AXES),
        P(FEEDER_AXES, TM_AXES),
        P(FEEDER_AXES, None),
        P(None, TM_AXES),
        P(),
        P(),
        rows,
        rows,
    )
    return jax.shard_map(
        per_device,
        mesh=fine,
        in_specs=placed,
        out_specs=(rows, rows, rows, P(FEEDER_AXES, TM_AXES)),
        check_vma=False,
    )
```

```python
import functools

import jax
import jax.numpy as jnp
from jax import lax
from jax.experimental import pallas as pl
from jax.experimental.pallas import tpu as pltpu
from jax.sharding import Mesh
from jax.sharding import PartitionSpec as P

LAGMAX = 1440
DATA_WEIGHT = 1.0 / 64.0
LAM_F = 0.1
LAM_X = 0.01
LAM_AR = 8.0
BETA_ONE = 0.9
BETA_TWO = 0.999
BIAS_FIRST = 1.0 - 0.9**8
BIAS_SECOND = 1.0 - 0.999**8
LEARNING_RATE = 0.05
ADAM_EPS = 1e-08

AXES = ("z_hi", "y", "z_lo", "x", "core")
FEEDER_AXES, TM_AXES = AXES[:2], AXES[2:]
PLANES, PLANE = 8, 8
TM = PLANES * PLANE
FEEDER = 8
SHARE = 48
BAND = 8
SPAN = 512
TILES = SPAN // 128
MAIN_ROWS = PLANES * SHARE // 2
BAND_ROWS = BAND * TILES
ROWS = MAIN_ROWS + 2 * BAND_ROWS
HOPS = 3
CHUNKS = (HOPS + 1) * TILES


def place_of(axes):
    place = 0
    for axis in axes:
        place = place * lax.axis_size(axis) + lax.axis_index(axis)
    return place


def main_kernel(observed, words, factor, time, keep, send, time_out, total, *, steps, planes):
    step = pl.program_id(0)
    factor_half = factor[...].astype(jnp.bfloat16)
    time_half = time[...].astype(jnp.bfloat16)
    predicted = lax.dot_general(
        factor_half, time_half, (((0,), (0,)), ((), ())), preferred_element_type=jnp.float32
    )
    word_count, span = words.shape[0], time.shape[1]
    spread = (
        lax.broadcasted_iota(jnp.int32, (word_count, span), 1) >> 3
        == lax.broadcasted_iota(jnp.int32, (word_count, span), 0)
    ).astype(jnp.float32).astype(jnp.bfloat16)
    wide = lax.dot_general(
        words[...].astype(jnp.float32).astype(jnp.bfloat16),
        spread,
        (((0,), (0,)), ((), ())),
        preferred_element_type=jnp.float32,
    ).astype(jnp.int32)
    bit = jnp.left_shift(1, lax.broadcasted_iota(jnp.int32, wide.shape, 1) & 7)
    residual = jnp.where(
        (wide & bit) != 0, predicted - observed[...].astype(jnp.float32), 0.0
    ).astype(jnp.bfloat16)
    rows = DATA_WEIGHT * lax.dot_general(
        residual, time_half, (((1,), (1,)), ((), ())), preferred_element_type=jnp.float32
    )
    half = SHARE // 2
    first = lax.axis_index("core") == 0
    for plane in range(planes):
        for x in range(PLANE // 2):
            pair = []
            for core in range(2):
                start = (plane * PLANE + 2 * x + core) * SHARE
                pair.append(
                    jnp.concatenate(
                        [rows[start : start + half], rows[start + half : start + SHARE]], axis=1
                    )
                )
            at = pl.ds(pl.multiple_of(x * MAIN_ROWS + (step * planes + plane) * half, 8), half)
            keep[at] = jnp.where(first, pair[0], pair[1])
            send[at] = jnp.where(first, pair[1], pair[0])
    term = jnp.dot(factor_half, residual, preferred_element_type=jnp.float32)

    @pl.when(step == 0)
    def _():
        total[...] = term
        own = time[pl.ds(pl.multiple_of(place_of(FEEDER_AXES) * BAND, BAND), BAND), :]
        for tile in range(TILES):
            at = PLANE // 2 * MAIN_ROWS + BAND * tile
            keep[at : at + BAND] = own[:, 128 * tile : 128 * tile + 128]
            send[at : at + BAND] = own[:, 128 * tile : 128 * tile + 128]

    @pl.when(step > 0)
    def _():
        total[...] = total[...] + term

    @pl.when(step == steps - 1)
    def _():
        z_hi = lax.axis_index("z_hi")
        for band in range(FEEDER):
            z, y = band >> 2, band & 3
            time_out[y, z_hi ^ z] = DATA_WEIGHT * total[BAND * band : BAND * band + BAND]


def main_terms(observed, words, factor, time, steps=4):
    feeders, span = observed.shape
    ranks, block = factor.shape[0], feeders // steps
    half_rows = PLANE // 2 * MAIN_ROWS + BAND_ROWS
    return pl.pallas_call(
        functools.partial(main_kernel, steps=steps, planes=PLANES // steps),
        grid=(steps,),
        in_specs=[
            pl.BlockSpec((block, span), lambda s: (s, 0)),
            pl.BlockSpec((words.shape[0], block), lambda s: (0, s)),
            pl.BlockSpec((ranks, block), lambda s: (0, s)),
            pl.BlockSpec((ranks, span), lambda s: (0, 0)),
        ],
        out_specs=[
            pl.BlockSpec((half_rows, 128), lambda s: (0, 0)),
            pl.BlockSpec((half_rows, 128), lambda s: (0, 0)),
            pl.BlockSpec((4, 2, BAND, span), lambda s: (0, 0, 0, 0)),
        ],
        scratch_shapes=[pltpu.VMEM((ranks, span), jnp.float32)],
        out_shape=[
            jax.ShapeDtypeStruct((half_rows, 128), jnp.float32),
            jax.ShapeDtypeStruct((half_rows, 128), jnp.float32),
            jax.ShapeDtypeStruct((4, 2, BAND, span), jnp.float32),
        ],
        cost_estimate=pl.CostEstimate(flops=805306368, bytes_accessed=6_000_000, transcendentals=0),
        compiler_params=pltpu.CompilerParams(vmem_limit_bytes=24 << 20),
        name="main_terms",
    )(*(pltpu.with_memory_space_constraint(a, pltpu.HBM) for a in (observed, words, factor, time)))


def pair_kernel(keep, got, out):
    first = lax.axis_index("core") == 0
    tail = PLANE // 2 * MAIN_ROWS
    mine, other = keep[tail:], got[tail:]
    for x in range(PLANE // 2):
        at = slice(x * MAIN_ROWS, (x + 1) * MAIN_ROWS)
        out[x, :MAIN_ROWS] = keep[at] + got[at]
        out[x, MAIN_ROWS : MAIN_ROWS + BAND_ROWS] = jnp.where(first, mine, other)
        out[x, MAIN_ROWS + BAND_ROWS :] = jnp.where(first, other, mine)


def pair_terms(keep, got):
    in_vmem = pl.BlockSpec(memory_space=pltpu.VMEM)
    return pl.pallas_call(
        pair_kernel,
        in_specs=[in_vmem, in_vmem],
        out_specs=in_vmem,
        out_shape=jax.ShapeDtypeStruct((PLANE // 2, ROWS, 128), jnp.float32),
        cost_estimate=pl.CostEstimate(flops=100_000, bytes_accessed=1_400_000, transcendentals=0),
        compiler_params=pltpu.CompilerParams(vmem_limit_bytes=8 << 20),
        name="pair_terms",
    )(keep, got)


def split_kernel(got, planes, passed):
    total = got[0, :MAIN_ROWS]
    for x in range(1, PLANE // 2):
        total = total + got[x, :MAIN_ROWS]
    half = SHARE // 2
    for z in range(PLANES):
        planes[z] = total[half * z : half * z + half]
    late = place_of(AXES[3:]) < PLANE // 2
    for span in range(HOPS):
        ends = []
        for source in (PLANE - HOPS + span, span):
            at = MAIN_ROWS + BAND_ROWS * (source & 1)
            ends.append(got[source >> 1, at : at + BAND_ROWS])
        passed[span] = jnp.where(late, ends[0], ends[1])


def split_terms(got):
    in_vmem = pl.BlockSpec(memory_space=pltpu.VMEM)
    return pl.pallas_call(
        split_kernel,
        in_specs=[in_vmem],
        out_specs=[in_vmem, in_vmem],
        out_shape=[
            jax.ShapeDtypeStruct((PLANES, SHARE // 2, 128), jnp.float32),
            jax.ShapeDtypeStruct((HOPS, BAND_ROWS, 128), jnp.float32),
        ],
        cost_estimate=pl.CostEstimate(flops=100_000, bytes_accessed=700_000, transcendentals=0),
        compiler_params=pltpu.CompilerParams(vmem_limit_bytes=8 << 20),
        name="split_terms",
    )(got)


def shifted_tiles(start, count, read):
    first, lane = start >> 7, start & 127
    back = (128 - lane) & 127
    rolled = [pltpu.roll(read(first + i), back, 1) for i in range(count + 1)]
    inside = lax.broadcasted_iota(jnp.int32, (BAND, 128), 1) < 128 - lane
    return [jnp.where(inside, rolled[i], rolled[i + 1]) for i in range(count)]


def ar_kernel(
    lags, weights, plane, beside, home, away, time_grad, spans, errors, weight_rows
):
    edge = HOPS * TILES
    for span in range(HOPS):
        for tile in range(TILES):
            value = beside[span, BAND * tile : BAND * tile + BAND]
            spans[span * TILES + tile] = value
            spans[edge + PLANE * TILES + span * TILES + tile] = value
    for span in range(PLANE):
        for tile in range(TILES):
            spans[edge + span * TILES + tile] = plane[span, BAND * tile : BAND * tile + BAND]
    weight_rows[...] = weights[...].T
    mine = weight_rows[pl.ds(pl.multiple_of(place_of(FEEDER_AXES) * BAND, BAND), BAND), :]
    own_tile = edge + place_of(AXES[3:]) * TILES
    own_column = own_tile * 128
    count = lags.shape[0]
    gains = [jnp.broadcast_to(mine[:, k : k + 1], (BAND, 128)) for k in range(count)]
    parts = [jnp.zeros((BAND, 128), jnp.float32) for _ in range(CHUNKS)]
    for k in range(count):
        moved = shifted_tiles(own_column - lags[k], CHUNKS, lambda i: spans[i])
        parts = [part + gains[k] * tile for part, tile in zip(parts, moved)]
    lane = lax.broadcasted_iota(jnp.int32, (BAND, 128), 1)
    first = place_of(TM_AXES) * SPAN
    for chunk in range(CHUNKS):
        column = first + 128 * chunk + lane
        inside = (column >= LAGMAX) & (column < TM * SPAN)
        errors[chunk] = jnp.where(inside, spans[own_tile + chunk] - parts[chunk], 0.0)
    errors[CHUNKS] = jnp.zeros((BAND, 128), jnp.float32)
    carried = [jnp.zeros((BAND, 128), jnp.float32) for _ in range(TILES)]
    for k in range(count):
        moved = shifted_tiles(lags[k], TILES, lambda i: errors[i])
        carried = [part + gains[k] * tile for part, tile in zip(carried, moved)]
    for tile in range(TILES):
        at = slice(128 * tile, 128 * tile + 128)
        time_grad[:, at] = (
            home[:, at]
            + away[:, at]
            + LAM_AR * (errors[tile] - carried[tile])
            + LAM_X * spans[own_tile + tile]
        )


def ar_terms(lags, weights, plane, beside, home, away):
    in_vmem = pl.BlockSpec(memory_space=pltpu.VMEM)
    in_smem = pl.BlockSpec(memory_space=pltpu.SMEM)
    tiles = (2 * HOPS + PLANE) * TILES
    return pl.pallas_call(
        ar_kernel,
        in_specs=[in_smem] + [in_vmem] * 5,
        out_specs=in_vmem,
        out_shape=jax.ShapeDtypeStruct((BAND, SPAN), jnp.float32),
        scratch_shapes=[
            pltpu.VMEM((tiles + 1, BAND, 128), jnp.float32),
            pltpu.VMEM((CHUNKS + 1, BAND, 128), jnp.float32),
            pltpu.VMEM(weights.shape[::-1], jnp.float32),
        ],
        cost_estimate=pl.CostEstimate(flops=2_000_000, bytes_accessed=400_000, transcendentals=0),
        compiler_params=pltpu.CompilerParams(vmem_limit_bytes=8 << 20),
        name="ar_terms",
    )(lags, weights, plane, beside, home, away)


def per_device(
    observed, mask_words, feeder_factor, time_factor, ar_weight, lags, moment_first, moment_second
):
    ranks = time_factor.shape[0]
    tm_place = lax.axis_index(TM_AXES)

    keep, send, time_part = main_terms(observed, mask_words.T, feeder_factor.T, time_factor)
    got = lax.ppermute(send, "core", [(0, 1), (1, 0)])
    bands = lax.all_to_all(time_part, "y", 0, 0, tiled=True)
    got = lax.all_to_all(pair_terms(keep, got), "x", 0, 0, tiled=True)
    bands = bands.sum(0)
    away = lax.ppermute(bands[1], "z_hi", [(0, 1), (1, 0)])

    planes, passed = split_terms(got)
    plane = got[:, MAIN_ROWS:].reshape(PLANE, BAND_ROWS, 128)
    pairs = [(t, t + PLANE) for t in range(TM - PLANE) if t % PLANE < PLANE // 2]
    pairs += [(t, t - PLANE) for t in range(PLANE, TM) if t % PLANE >= PLANE // 2]
    beside = lax.ppermute(passed, TM_AXES, pairs)
    share = lax.all_to_all(planes, "z_lo", 0, 0, tiled=True)
    share = share.sum(0)
    time_grad = ar_terms(lags, ar_weight, plane, beside, bands[0], away)

    grad_share = jnp.concatenate([share[:, :ranks], share[:, ranks:]], axis=0)
    own_factor = lax.dynamic_slice_in_dim(feeder_factor, tm_place * SHARE, SHARE, 0)
    factor_grad = grad_share + LAM_F * own_factor
    new_first = BETA_ONE * moment_first + (1.0 - BETA_ONE) * factor_grad
    new_second = BETA_TWO * moment_second + (1.0 - BETA_TWO) * factor_grad * factor_grad
    update = (
        LEARNING_RATE * (new_first / BIAS_FIRST) / (jnp.sqrt(new_second / BIAS_SECOND) + ADAM_EPS)
    )
    return (own_factor - update, new_first, new_second, time_grad)


def solution(mesh):
    fine = Mesh(mesh.devices.reshape(2, 4, 8, 4, 2), AXES)
    rows = P(AXES, None)
    placed = (
        P(FEEDER_AXES, TM_AXES),
        P(FEEDER_AXES, TM_AXES),
        P(FEEDER_AXES, None),
        P(None, TM_AXES),
        P(),
        P(),
        rows,
        rows,
    )
    return jax.shard_map(
        per_device,
        mesh=fine,
        in_specs=placed,
        out_specs=(rows, rows, rows, P(FEEDER_AXES, TM_AXES)),
        check_vma=False,
    )
```

```python
import functools

import jax
import jax.numpy as jnp
from jax import lax
from jax.experimental import pallas as pl
from jax.experimental.pallas import tpu as pltpu
from jax.sharding import Mesh
from jax.sharding import PartitionSpec as P

LAGMAX = 1440
DATA_WEIGHT = 1.0 / 64.0
LAM_F = 0.1
LAM_X = 0.01
LAM_AR = 8.0
BETA_ONE = 0.9
BETA_TWO = 0.999
BIAS_FIRST = 1.0 - 0.9**8
BIAS_SECOND = 1.0 - 0.999**8
LEARNING_RATE = 0.05
ADAM_EPS = 1e-08

AXES = ("z_hi", "y", "z_lo", "x", "core")
FEEDER_AXES, TM_AXES = AXES[:2], AXES[2:]
PLANES, PLANE = 8, 8
TM = PLANES * PLANE
FEEDER = 8
SHARE = 48
BAND = 8
SPAN = 512
TILES = SPAN // 128
MAIN_ROWS = PLANES * SHARE // 2
BAND_ROWS = BAND * TILES
ROWS = MAIN_ROWS + 2 * BAND_ROWS
HOPS = 3
CHUNKS = (HOPS + 1) * TILES


def place_of(axes):
    place = 0
    for axis in axes:
        place = place * lax.axis_size(axis) + lax.axis_index(axis)
    return place


def main_kernel(observed, words, factor, time, keep, send, time_out, total, *, steps, planes):
    step = pl.program_id(0)
    factor_half = factor[...].astype(jnp.bfloat16)
    time_half = time[...].astype(jnp.bfloat16)
    predicted = lax.dot_general(
        factor_half, time_half, (((0,), (0,)), ((), ())), preferred_element_type=jnp.float32
    )
    word_count, span = words.shape[0], time.shape[1]
    spread = (
        lax.broadcasted_iota(jnp.int32, (word_count, span), 1) >> 3
        == lax.broadcasted_iota(jnp.int32, (word_count, span), 0)
    )
    power = 1.0 / jnp.left_shift(2, lax.broadcasted_iota(jnp.int32, (1, span), 1) & 7).astype(jnp.float32)
    spread = jnp.where(spread, power, 0.0).astype(jnp.bfloat16)
    wide = lax.dot_general(
        words[...].astype(jnp.float32).astype(jnp.bfloat16),
        spread,
        (((0,), (0,)), ((), ())),
        preferred_element_type=jnp.float32,
    )
    residual = jnp.where(
        wide - jnp.floor(wide) >= 0.5, predicted - observed[...].astype(jnp.float32), 0.0
    ).astype(jnp.bfloat16)
    rows = DATA_WEIGHT * lax.dot_general(
        residual, time_half, (((1,), (1,)), ((), ())), preferred_element_type=jnp.float32
    )
    half = SHARE // 2
    first = lax.axis_index("core") == 0
    for plane in range(planes):
        for x in range(PLANE // 2):
            pair = []
            for core in range(2):
                start = (plane * PLANE + 2 * x + core) * SHARE
                pair.append(
                    jnp.concatenate(
                        [rows[start : start + half], rows[start + half : start + SHARE]], axis=1
                    )
                )
            at = pl.ds(pl.multiple_of(x * MAIN_ROWS + (step * planes + plane) * half, 8), half)
            keep[at] = jnp.where(first, pair[0], pair[1])
            send[at] = jnp.where(first, pair[1], pair[0])
    term = jnp.dot(factor_half, residual, preferred_element_type=jnp.float32)

    @pl.when(step == 0)
    def _():
        total[...] = term
        own = time[pl.ds(pl.multiple_of(place_of(FEEDER_AXES) * BAND, BAND), BAND), :]
        for tile in range(TILES):
            at = PLANE // 2 * MAIN_ROWS + BAND * tile
            keep[at : at + BAND] = own[:, 128 * tile : 128 * tile + 128]
            send[at : at + BAND] = own[:, 128 * tile : 128 * tile + 128]

    @pl.when(step > 0)
    def _():
        total[...] = total[...] + term

    @pl.when(step == steps - 1)
    def _():
        z_hi = lax.axis_index("z_hi")
        for band in range(FEEDER):
            z, y = band >> 2, band & 3
            time_out[y, z_hi ^ z] = DATA_WEIGHT * total[BAND * band : BAND * band + BAND]


def main_terms(observed, words, factor, time, steps=4):
    feeders, span = observed.shape
    ranks, block = factor.shape[0], feeders // steps
    half_rows = PLANE // 2 * MAIN_ROWS + BAND_ROWS
    return pl.pallas_call(
        functools.partial(main_kernel, steps=steps, planes=PLANES // steps),
        grid=(steps,),
        in_specs=[
            pl.BlockSpec((block, span), lambda s: (s, 0)),
            pl.BlockSpec((words.shape[0], block), lambda s: (0, s)),
            pl.BlockSpec((ranks, block), lambda s: (0, s)),
            pl.BlockSpec((ranks, span), lambda s: (0, 0)),
        ],
        out_specs=[
            pl.BlockSpec((half_rows, 128), lambda s: (0, 0)),
            pl.BlockSpec((half_rows, 128), lambda s: (0, 0)),
            pl.BlockSpec((4, 2, BAND, span), lambda s: (0, 0, 0, 0)),
        ],
        scratch_shapes=[pltpu.VMEM((ranks, span), jnp.float32)],
        out_shape=[
            jax.ShapeDtypeStruct((half_rows, 128), jnp.float32),
            jax.ShapeDtypeStruct((half_rows, 128), jnp.float32),
            jax.ShapeDtypeStruct((4, 2, BAND, span), jnp.float32),
        ],
        cost_estimate=pl.CostEstimate(flops=805306368, bytes_accessed=6_000_000, transcendentals=0),
        compiler_params=pltpu.CompilerParams(vmem_limit_bytes=24 << 20),
        name="main_terms",
    )(*(pltpu.with_memory_space_constraint(a, pltpu.HBM) for a in (observed, words, factor, time)))


def pair_kernel(keep, got, out):
    first = lax.axis_index("core") == 0
    tail = PLANE // 2 * MAIN_ROWS
    mine, other = keep[tail:], got[tail:]
    for x in range(PLANE // 2):
        at = slice(x * MAIN_ROWS, (x + 1) * MAIN_ROWS)
        out[x, :MAIN_ROWS] = keep[at] + got[at]
        out[x, MAIN_ROWS : MAIN_ROWS + BAND_ROWS] = jnp.where(first, mine, other)
        out[x, MAIN_ROWS + BAND_ROWS :] = jnp.where(first, other, mine)


def pair_terms(keep, got):
    in_vmem = pl.BlockSpec(memory_space=pltpu.VMEM)
    return pl.pallas_call(
        pair_kernel,
        in_specs=[in_vmem, in_vmem],
        out_specs=in_vmem,
        out_shape=jax.ShapeDtypeStruct((PLANE // 2, ROWS, 128), jnp.float32),
        cost_estimate=pl.CostEstimate(flops=100_000, bytes_accessed=1_400_000, transcendentals=0),
        compiler_params=pltpu.CompilerParams(vmem_limit_bytes=8 << 20),
        name="pair_terms",
    )(keep, got)


def split_kernel(got, planes, passed):
    total = got[0, :MAIN_ROWS]
    for x in range(1, PLANE // 2):
        total = total + got[x, :MAIN_ROWS]
    half = SHARE // 2
    for z in range(PLANES):
        planes[z] = total[half * z : half * z + half]
    late = place_of(AXES[3:]) < PLANE // 2
    for span in range(HOPS):
        ends = []
        for source in (PLANE - HOPS + span, span):
            at = MAIN_ROWS + BAND_ROWS * (source & 1)
            ends.append(got[source >> 1, at : at + BAND_ROWS])
        passed[span] = jnp.where(late, ends[0], ends[1])


def split_terms(got):
    in_vmem = pl.BlockSpec(memory_space=pltpu.VMEM)
    return pl.pallas_call(
        split_kernel,
        in_specs=[in_vmem],
        out_specs=[in_vmem, in_vmem],
        out_shape=[
            jax.ShapeDtypeStruct((PLANES, SHARE // 2, 128), jnp.float32),
            jax.ShapeDtypeStruct((HOPS, BAND_ROWS, 128), jnp.float32),
        ],
        cost_estimate=pl.CostEstimate(flops=100_000, bytes_accessed=700_000, transcendentals=0),
        compiler_params=pltpu.CompilerParams(vmem_limit_bytes=8 << 20),
        name="split_terms",
    )(got)


def shifted_tiles(start, count, read):
    first, lane = start >> 7, start & 127
    back = (128 - lane) & 127
    rolled = [pltpu.roll(read(first + i), back, 1) for i in range(count + 1)]
    inside = lax.broadcasted_iota(jnp.int32, (BAND, 128), 1) < 128 - lane
    return [jnp.where(inside, rolled[i], rolled[i + 1]) for i in range(count)]


def ar_kernel(
    lags, weights, plane, beside, home, away, time_grad, spans, errors, weight_rows
):
    edge = HOPS * TILES
    for span in range(HOPS):
        for tile in range(TILES):
            value = beside[span, BAND * tile : BAND * tile + BAND]
            spans[span * TILES + tile] = value
            spans[edge + PLANE * TILES + span * TILES + tile] = value
    for span in range(PLANE):
        for tile in range(TILES):
            spans[edge + span * TILES + tile] = plane[span, BAND * tile : BAND * tile + BAND]
    weight_rows[...] = weights[...].T
    mine = weight_rows[pl.ds(pl.multiple_of(place_of(FEEDER_AXES) * BAND, BAND), BAND), :]
    own_tile = edge + place_of(AXES[3:]) * TILES
    own_column = own_tile * 128
    count = lags.shape[0]
    gains = [jnp.broadcast_to(mine[:, k : k + 1], (BAND, 128)) for k in range(count)]
    parts = [jnp.zeros((BAND, 128), jnp.float32) for _ in range(CHUNKS)]
    for k in range(count):
        moved = shifted_tiles(own_column - lags[k], CHUNKS, lambda i: spans[i])
        parts = [part + gains[k] * tile for part, tile in zip(parts, moved)]
    lane = lax.broadcasted_iota(jnp.int32, (BAND, 128), 1)
    first = place_of(TM_AXES) * SPAN
    for chunk in range(CHUNKS):
        column = first + 128 * chunk + lane
        inside = (column >= LAGMAX) & (column < TM * SPAN)
        errors[chunk] = jnp.where(inside, spans[own_tile + chunk] - parts[chunk], 0.0)
    errors[CHUNKS] = jnp.zeros((BAND, 128), jnp.float32)
    carried = [jnp.zeros((BAND, 128), jnp.float32) for _ in range(TILES)]
    for k in range(count):
        moved = shifted_tiles(lags[k], TILES, lambda i: errors[i])
        carried = [part + gains[k] * tile for part, tile in zip(carried, moved)]
    for tile in range(TILES):
        at = slice(128 * tile, 128 * tile + 128)
        time_grad[:, at] = (
            home[:, at]
            + away[:, at]
            + LAM_AR * (errors[tile] - carried[tile])
            + LAM_X * spans[own_tile + tile]
        )


def ar_terms(lags, weights, plane, beside, home, away):
    in_vmem = pl.BlockSpec(memory_space=pltpu.VMEM)
    in_smem = pl.BlockSpec(memory_space=pltpu.SMEM)
    tiles = (2 * HOPS + PLANE) * TILES
    return pl.pallas_call(
        ar_kernel,
        in_specs=[in_smem] + [in_vmem] * 5,
        out_specs=in_vmem,
        out_shape=jax.ShapeDtypeStruct((BAND, SPAN), jnp.float32),
        scratch_shapes=[
            pltpu.VMEM((tiles + 1, BAND, 128), jnp.float32),
            pltpu.VMEM((CHUNKS + 1, BAND, 128), jnp.float32),
            pltpu.VMEM(weights.shape[::-1], jnp.float32),
        ],
        cost_estimate=pl.CostEstimate(flops=2_000_000, bytes_accessed=400_000, transcendentals=0),
        compiler_params=pltpu.CompilerParams(vmem_limit_bytes=8 << 20),
        name="ar_terms",
    )(lags, weights, plane, beside, home, away)


def per_device(
    observed, mask_words, feeder_factor, time_factor, ar_weight, lags, moment_first, moment_second
):
    ranks = time_factor.shape[0]
    tm_place = lax.axis_index(TM_AXES)

    keep, send, time_part = main_terms(observed, mask_words.T, feeder_factor.T, time_factor)
    got = lax.ppermute(send, "core", [(0, 1), (1, 0)])
    own_factor = lax.dynamic_slice_in_dim(feeder_factor, tm_place * SHARE, SHARE, 0)
    bands = lax.all_to_all(time_part, "y", 0, 0, tiled=True)
    got = lax.all_to_all(pair_terms(keep, got), "x", 0, 0, tiled=True)
    bands = bands.sum(0)
    away = lax.ppermute(bands[1], "z_hi", [(0, 1), (1, 0)])

    planes, passed = split_terms(got)
    plane = got[:, MAIN_ROWS:].reshape(PLANE, BAND_ROWS, 128)
    pairs = [(t, t + PLANE) for t in range(TM - PLANE) if t % PLANE < PLANE // 2]
    pairs += [(t, t - PLANE) for t in range(PLANE, TM) if t % PLANE >= PLANE // 2]
    beside = lax.ppermute(passed, TM_AXES, pairs)
    share = lax.all_to_all(planes, "z_lo", 0, 0, tiled=True)
    share = share.sum(0)
    time_grad = ar_terms(lags, ar_weight, plane, beside, bands[0], away)

    grad_share = jnp.concatenate([share[:, :ranks], share[:, ranks:]], axis=0)
    factor_grad = grad_share + LAM_F * own_factor
    new_first = BETA_ONE * moment_first + (1.0 - BETA_ONE) * factor_grad
    new_second = BETA_TWO * moment_second + (1.0 - BETA_TWO) * factor_grad * factor_grad
    update = (
        LEARNING_RATE * (new_first / BIAS_FIRST) / (jnp.sqrt(new_second / BIAS_SECOND) + ADAM_EPS)
    )
    return (own_factor - update, new_first, new_second, time_grad)


def solution(mesh):
    fine = Mesh(mesh.devices.reshape(2, 4, 8, 4, 2), AXES)
    rows = P(AXES, None)
    placed = (
        P(FEEDER_AXES, TM_AXES),
        P(FEEDER_AXES, TM_AXES),
        P(FEEDER_AXES, None),
        P(None, TM_AXES),
        P(),
        P(),
        rows,
        rows,
    )
    return jax.shard_map(
        per_device,
        mesh=fine,
        in_specs=placed,
        out_specs=(rows, rows, rows, P(FEEDER_AXES, TM_AXES)),
        check_vma=False,
    )
```

```python
import functools

import jax
import jax.numpy as jnp
from jax import lax
from jax.experimental import pallas as pl
from jax.experimental.pallas import tpu as pltpu
from jax.sharding import Mesh
from jax.sharding import PartitionSpec as P

LAGMAX = 1440
DATA_WEIGHT = 1.0 / 64.0
LAM_F = 0.1
LAM_X = 0.01
LAM_AR = 8.0
BETA_ONE = 0.9
BETA_TWO = 0.999
BIAS_FIRST = 1.0 - 0.9**8
BIAS_SECOND = 1.0 - 0.999**8
LEARNING_RATE = 0.05
ADAM_EPS = 1e-08

AXES = ("z_hi", "y", "z_lo", "x", "core")
FEEDER_AXES, TM_AXES = AXES[:2], AXES[2:]
PLANES, PLANE = 8, 8
TM = PLANES * PLANE
SHARE = 48
BAND = 8
SPAN = 512
TILES = SPAN // 128
MAIN_ROWS = PLANES * SHARE // 2
BAND_ROWS = BAND * TILES
ROWS = MAIN_ROWS + 2 * BAND_ROWS
HOPS = 3
CHUNKS = (HOPS + 1) * TILES


def gray(place):
    return place ^ (place >> 1)


def place_of(axes):
    place = 0
    for axis in axes:
        place = place * lax.axis_size(axis) + lax.axis_index(axis)
    return place


def main_kernel(
    observed, words, factor, time, keep, send, time_keep, time_send, total, *, steps, planes
):
    step = pl.program_id(0)
    factor_half = factor[...].astype(jnp.bfloat16)
    time_half = time[...].astype(jnp.bfloat16)
    predicted = lax.dot_general(
        factor_half, time_half, (((0,), (0,)), ((), ())), preferred_element_type=jnp.float32
    )
    word_count, span = words.shape[0], time.shape[1]
    spread = (
        lax.broadcasted_iota(jnp.int32, (word_count, span), 1) >> 3
        == lax.broadcasted_iota(jnp.int32, (word_count, span), 0)
    )
    power = 1.0 / jnp.left_shift(2, lax.broadcasted_iota(jnp.int32, (1, span), 1) & 7).astype(jnp.float32)
    spread = jnp.where(spread, power, 0.0).astype(jnp.bfloat16)
    wide = lax.dot_general(
        words[...].astype(jnp.float32).astype(jnp.bfloat16),
        spread,
        (((0,), (0,)), ((), ())),
        preferred_element_type=jnp.float32,
    )
    residual = jnp.where(
        wide - jnp.floor(wide) >= 0.5, predicted - observed[...].astype(jnp.float32), 0.0
    ).astype(jnp.bfloat16)
    rows = DATA_WEIGHT * lax.dot_general(
        residual, time_half, (((1,), (1,)), ((), ())), preferred_element_type=jnp.float32
    )
    half = SHARE // 2
    first = lax.axis_index("core") == 0
    for plane in range(planes):
        for x in range(PLANE // 2):
            pair = []
            for core in range(2):
                start = (plane * PLANE + 2 * x + core) * SHARE
                pair.append(
                    jnp.concatenate(
                        [rows[start : start + half], rows[start + half : start + SHARE]], axis=1
                    )
                )
            at = pl.ds(pl.multiple_of(x * MAIN_ROWS + (step * planes + plane) * half, 8), half)
            keep[at] = jnp.where(first, pair[0], pair[1])
            send[at] = jnp.where(first, pair[1], pair[0])
    term = jnp.dot(factor_half, residual, preferred_element_type=jnp.float32)

    @pl.when(step == 0)
    def _():
        total[...] = term
        own = time[pl.ds(pl.multiple_of(place_of(FEEDER_AXES) * BAND, BAND), BAND), :]
        for tile in range(TILES):
            at = PLANE // 2 * MAIN_ROWS + BAND * tile
            keep[at : at + BAND] = own[:, 128 * tile : 128 * tile + 128]
            send[at : at + BAND] = own[:, 128 * tile : 128 * tile + 128]

    @pl.when(step > 0)
    def _():
        total[...] = total[...] + term

    @pl.when(step == steps - 1)
    def _():
        z_hi, y_ring = lax.axis_index("z_hi"), gray(lax.axis_index("y"))
        for near in range(4):
            far = near ^ y_ring
            for z in range(2):
                band = (z ^ z_hi) * 4 + (far ^ (far >> 1))
                rows_out = DATA_WEIGHT * total[pl.ds(pl.multiple_of(band * BAND, BAND), BAND), :]
                if near & 1:
                    time_send[near >> 1, z] = rows_out
                else:
                    time_keep[near >> 1, z] = rows_out


def main_terms(observed, words, factor, time, steps=4):
    feeders, span = observed.shape
    ranks, block = factor.shape[0], feeders // steps
    half_rows = PLANE // 2 * MAIN_ROWS + BAND_ROWS
    return pl.pallas_call(
        functools.partial(main_kernel, steps=steps, planes=PLANES // steps),
        grid=(steps,),
        in_specs=[
            pl.BlockSpec((block, span), lambda s: (s, 0)),
            pl.BlockSpec((words.shape[0], block), lambda s: (0, s)),
            pl.BlockSpec((ranks, block), lambda s: (0, s)),
            pl.BlockSpec((ranks, span), lambda s: (0, 0)),
        ],
        out_specs=[
            pl.BlockSpec((half_rows, 128), lambda s: (0, 0)),
            pl.BlockSpec((half_rows, 128), lambda s: (0, 0)),
            pl.BlockSpec((2, 2, BAND, span), lambda s: (0, 0, 0, 0)),
            pl.BlockSpec((2, 2, BAND, span), lambda s: (0, 0, 0, 0)),
        ],
        scratch_shapes=[pltpu.VMEM((ranks, span), jnp.float32)],
        out_shape=[
            jax.ShapeDtypeStruct((half_rows, 128), jnp.float32),
            jax.ShapeDtypeStruct((half_rows, 128), jnp.float32),
            jax.ShapeDtypeStruct((2, 2, BAND, span), jnp.float32),
            jax.ShapeDtypeStruct((2, 2, BAND, span), jnp.float32),
        ],
        cost_estimate=pl.CostEstimate(flops=805306368, bytes_accessed=6_000_000, transcendentals=0),
        compiler_params=pltpu.CompilerParams(vmem_limit_bytes=24 << 20),
        name="main_terms",
    )(*(pltpu.with_memory_space_constraint(a, pltpu.HBM) for a in (observed, words, factor, time)))


def pair_kernel(keep, got, out):
    first = lax.axis_index("core") == 0
    tail = PLANE // 2 * MAIN_ROWS
    mine, other = keep[tail:], got[tail:]
    for x in range(PLANE // 2):
        at = slice(x * MAIN_ROWS, (x + 1) * MAIN_ROWS)
        out[x, :MAIN_ROWS] = keep[at] + got[at]
        out[x, MAIN_ROWS : MAIN_ROWS + BAND_ROWS] = jnp.where(first, mine, other)
        out[x, MAIN_ROWS + BAND_ROWS :] = jnp.where(first, other, mine)


def pair_terms(keep, got):
    in_vmem = pl.BlockSpec(memory_space=pltpu.VMEM)
    return pl.pallas_call(
        pair_kernel,
        in_specs=[in_vmem, in_vmem],
        out_specs=in_vmem,
        out_shape=jax.ShapeDtypeStruct((PLANE // 2, ROWS, 128), jnp.float32),
        cost_estimate=pl.CostEstimate(flops=100_000, bytes_accessed=1_400_000, transcendentals=0),
        compiler_params=pltpu.CompilerParams(vmem_limit_bytes=8 << 20),
        name="pair_terms",
    )(keep, got)


def split_kernel(got, planes, passed):
    total = got[0, :MAIN_ROWS]
    for x in range(1, PLANE // 2):
        total = total + got[x, :MAIN_ROWS]
    half = SHARE // 2
    for z in range(PLANES):
        planes[z] = total[half * z : half * z + half]
    late = place_of(AXES[3:]) < PLANE // 2
    for span in range(HOPS):
        ends = []
        for source in (PLANE - HOPS + span, span):
            at = MAIN_ROWS + BAND_ROWS * (source & 1)
            ends.append(got[source >> 1, at : at + BAND_ROWS])
        passed[span] = jnp.where(late, ends[0], ends[1])


def split_terms(got):
    in_vmem = pl.BlockSpec(memory_space=pltpu.VMEM)
    return pl.pallas_call(
        split_kernel,
        in_specs=[in_vmem],
        out_specs=[in_vmem, in_vmem],
        out_shape=[
            jax.ShapeDtypeStruct((PLANES, SHARE // 2, 128), jnp.float32),
            jax.ShapeDtypeStruct((HOPS, BAND_ROWS, 128), jnp.float32),
        ],
        cost_estimate=pl.CostEstimate(flops=100_000, bytes_accessed=700_000, transcendentals=0),
        compiler_params=pltpu.CompilerParams(vmem_limit_bytes=8 << 20),
        name="split_terms",
    )(got)


def shifted_tiles(start, count, read):
    first, lane = start >> 7, start & 127
    back = (128 - lane) & 127
    rolled = [pltpu.roll(read(first + i), back, 1) for i in range(count + 1)]
    inside = lax.broadcasted_iota(jnp.int32, (BAND, 128), 1) < 128 - lane
    return [jnp.where(inside, rolled[i], rolled[i + 1]) for i in range(count)]


def ar_kernel(
    lags, weights, plane, beside, home, away, time_grad, spans, errors, weight_rows
):
    edge = HOPS * TILES
    for span in range(HOPS):
        for tile in range(TILES):
            value = beside[span, BAND * tile : BAND * tile + BAND]
            spans[span * TILES + tile] = value
            spans[edge + PLANE * TILES + span * TILES + tile] = value
    for span in range(PLANE):
        for tile in range(TILES):
            spans[edge + span * TILES + tile] = plane[span, BAND * tile : BAND * tile + BAND]
    weight_rows[...] = weights[...].T
    mine = weight_rows[pl.ds(pl.multiple_of(place_of(FEEDER_AXES) * BAND, BAND), BAND), :]
    own_tile = edge + place_of(AXES[3:]) * TILES
    own_column = own_tile * 128
    count = lags.shape[0]
    gains = [jnp.broadcast_to(mine[:, k : k + 1], (BAND, 128)) for k in range(count)]
    parts = [jnp.zeros((BAND, 128), jnp.float32) for _ in range(CHUNKS)]
    for k in range(count):
        moved = shifted_tiles(own_column - lags[k], CHUNKS, lambda i: spans[i])
        parts = [part + gains[k] * tile for part, tile in zip(parts, moved)]
    lane = lax.broadcasted_iota(jnp.int32, (BAND, 128), 1)
    first = place_of(TM_AXES) * SPAN
    for chunk in range(CHUNKS):
        column = first + 128 * chunk + lane
        inside = (column >= LAGMAX) & (column < TM * SPAN)
        errors[chunk] = jnp.where(inside, spans[own_tile + chunk] - parts[chunk], 0.0)
    errors[CHUNKS] = jnp.zeros((BAND, 128), jnp.float32)
    carried = [jnp.zeros((BAND, 128), jnp.float32) for _ in range(TILES)]
    for k in range(count):
        moved = shifted_tiles(lags[k], TILES, lambda i: errors[i])
        carried = [part + gains[k] * tile for part, tile in zip(carried, moved)]
    for tile in range(TILES):
        at = slice(128 * tile, 128 * tile + 128)
        time_grad[:, at] = (
            home[:, at]
            + away[:, at]
            + LAM_AR * (errors[tile] - carried[tile])
            + LAM_X * spans[own_tile + tile]
        )


def ar_terms(lags, weights, plane, beside, home, away):
    in_vmem = pl.BlockSpec(memory_space=pltpu.VMEM)
    in_smem = pl.BlockSpec(memory_space=pltpu.SMEM)
    tiles = (2 * HOPS + PLANE) * TILES
    return pl.pallas_call(
        ar_kernel,
        in_specs=[in_smem] + [in_vmem] * 5,
        out_specs=in_vmem,
        out_shape=jax.ShapeDtypeStruct((BAND, SPAN), jnp.float32),
        scratch_shapes=[
            pltpu.VMEM((tiles + 1, BAND, 128), jnp.float32),
            pltpu.VMEM((CHUNKS + 1, BAND, 128), jnp.float32),
            pltpu.VMEM(weights.shape[::-1], jnp.float32),
        ],
        cost_estimate=pl.CostEstimate(flops=2_000_000, bytes_accessed=400_000, transcendentals=0),
        compiler_params=pltpu.CompilerParams(vmem_limit_bytes=8 << 20),
        name="ar_terms",
    )(lags, weights, plane, beside, home, away)


def per_device(
    observed, mask_words, feeder_factor, time_factor, ar_weight, lags, moment_first, moment_second
):
    ranks = time_factor.shape[0]
    tm_place = lax.axis_index(TM_AXES)

    keep, send, bands, sent_bands = main_terms(observed, mask_words.T, feeder_factor.T, time_factor)
    got = lax.ppermute(send, "core", [(0, 1), (1, 0)])
    own_factor = lax.dynamic_slice_in_dim(feeder_factor, tm_place * SHARE, SHARE, 0)
    bands = bands + lax.ppermute(sent_bands, "y", [(0, 1), (1, 0), (2, 3), (3, 2)])
    pair = pair_terms(keep, got)
    bands = bands[0] + lax.ppermute(bands[1], "y", [(0, 3), (3, 0), (1, 2), (2, 1)])
    got = lax.all_to_all(pair, "x", 0, 0, tiled=True)
    away = lax.ppermute(bands[1], "z_hi", [(0, 1), (1, 0)])

    planes, passed = split_terms(got)
    plane = got[:, MAIN_ROWS:].reshape(PLANE, BAND_ROWS, 128)
    pairs = [(t, t + PLANE) for t in range(TM - PLANE) if t % PLANE < PLANE // 2]
    pairs += [(t, t - PLANE) for t in range(PLANE, TM) if t % PLANE >= PLANE // 2]
    beside = lax.ppermute(passed, TM_AXES, pairs)
    share = lax.all_to_all(planes, "z_lo", 0, 0, tiled=True)
    share = share.sum(0)
    time_grad = ar_terms(lags, ar_weight, plane, beside, bands[0], away)

    grad_share = jnp.concatenate([share[:, :ranks], share[:, ranks:]], axis=0)
    factor_grad = grad_share + LAM_F * own_factor
    new_first = BETA_ONE * moment_first + (1.0 - BETA_ONE) * factor_grad
    new_second = BETA_TWO * moment_second + (1.0 - BETA_TWO) * factor_grad * factor_grad
    update = (
        LEARNING_RATE * (new_first / BIAS_FIRST) / (jnp.sqrt(new_second / BIAS_SECOND) + ADAM_EPS)
    )
    return (own_factor - update, new_first, new_second, time_grad)


def solution(mesh):
    fine = Mesh(mesh.devices.reshape(2, 4, 8, 4, 2), AXES)
    rows = P(AXES, None)
    placed = (
        P(FEEDER_AXES, TM_AXES),
        P(FEEDER_AXES, TM_AXES),
        P(FEEDER_AXES, None),
        P(None, TM_AXES),
        P(),
        P(),
        rows,
        rows,
    )
    return jax.shard_map(
        per_device,
        mesh=fine,
        in_specs=placed,
        out_specs=(rows, rows, rows, P(FEEDER_AXES, TM_AXES)),
        check_vma=False,
    )
```

```python
import functools

import jax
import jax.numpy as jnp
from jax import lax
from jax.experimental import pallas as pl
from jax.experimental.pallas import tpu as pltpu
from jax.sharding import Mesh
from jax.sharding import PartitionSpec as P

LAGMAX = 1440
DATA_WEIGHT = 1.0 / 64.0
LAM_F = 0.1
LAM_X = 0.01
LAM_AR = 8.0
BETA_ONE = 0.9
BETA_TWO = 0.999
BIAS_FIRST = 1.0 - 0.9**8
BIAS_SECOND = 1.0 - 0.999**8
LEARNING_RATE = 0.05
ADAM_EPS = 1e-08

AXES = ("z_hi", "y", "z_lo", "x", "core")
FEEDER_AXES, TM_AXES = AXES[:2], AXES[2:]
PLANES, PLANE = 8, 8
TM = PLANES * PLANE
SHARE = 48
BAND = 8
SPAN = 512
TILES = SPAN // 128
MAIN_ROWS = PLANES * SHARE // 2
BAND_ROWS = BAND * TILES
ROWS = MAIN_ROWS + 2 * BAND_ROWS
HOPS = 3
CHUNKS = (HOPS + 1) * TILES


def gray(place):
    return place ^ (place >> 1)


def place_of(axes):
    place = 0
    for axis in axes:
        place = place * lax.axis_size(axis) + lax.axis_index(axis)
    return place


def main_kernel(
    observed, words, factor, time, keep, send, time_keep, time_send, total, *, steps, planes
):
    step = pl.program_id(0)
    factor_half = factor[...].astype(jnp.bfloat16)
    time_half = time[...].astype(jnp.bfloat16)
    predicted = lax.dot_general(
        factor_half, time_half, (((0,), (0,)), ((), ())), preferred_element_type=jnp.float32
    )
    word_count, span = words.shape[0], time.shape[1]
    spread = (
        lax.broadcasted_iota(jnp.int32, (word_count, span), 1) >> 3
        == lax.broadcasted_iota(jnp.int32, (word_count, span), 0)
    )
    power = 1.0 / jnp.left_shift(2, lax.broadcasted_iota(jnp.int32, (1, span), 1) & 7).astype(jnp.float32)
    spread = jnp.where(spread, power, 0.0).astype(jnp.bfloat16)
    wide = lax.dot_general(
        words[...].astype(jnp.float32).astype(jnp.bfloat16),
        spread,
        (((0,), (0,)), ((), ())),
        preferred_element_type=jnp.float32,
    )
    residual = jnp.where(
        wide - jnp.floor(wide) >= 0.5, predicted - observed[...].astype(jnp.float32), 0.0
    ).astype(jnp.bfloat16)
    rows = DATA_WEIGHT * lax.dot_general(
        residual, time_half, (((1,), (1,)), ((), ())), preferred_element_type=jnp.float32
    )
    half = SHARE // 2
    first = lax.axis_index("core") == 0
    for plane in range(planes):
        for x in range(PLANE // 2):
            pair = []
            for core in range(2):
                start = (plane * PLANE + 2 * x + core) * SHARE
                pair.append(
                    jnp.concatenate(
                        [rows[start : start + half], rows[start + half : start + SHARE]], axis=1
                    )
                )
            at = pl.ds(pl.multiple_of(x * MAIN_ROWS + (step * planes + plane) * half, 8), half)
            keep[at] = jnp.where(first, pair[0], pair[1])
            send[at] = jnp.where(first, pair[1], pair[0])
    term = jnp.dot(factor_half, residual, preferred_element_type=jnp.float32)

    @pl.when(step == 0)
    def _():
        total[...] = term
        own = time[pl.ds(pl.multiple_of(place_of(FEEDER_AXES) * BAND, BAND), BAND), :]
        for tile in range(TILES):
            at = PLANE // 2 * MAIN_ROWS + BAND * tile
            keep[at : at + BAND] = own[:, 128 * tile : 128 * tile + 128]
            send[at : at + BAND] = own[:, 128 * tile : 128 * tile + 128]

    @pl.when(step > 0)
    def _():
        total[...] = total[...] + term

    @pl.when(step == steps - 1)
    def _():
        z_hi, y_ring = lax.axis_index("z_hi"), gray(lax.axis_index("y"))
        for near in range(4):
            far = near ^ y_ring
            for z in range(2):
                band = (z ^ z_hi) * 4 + (far ^ (far >> 1))
                rows_out = DATA_WEIGHT * total[pl.ds(pl.multiple_of(band * BAND, BAND), BAND), :]
                if near & 1:
                    time_send[near >> 1, z] = rows_out
                else:
                    time_keep[near >> 1, z] = rows_out


def main_terms(observed, words, factor, time, steps=4):
    feeders, span = observed.shape
    ranks, block = factor.shape[0], feeders // steps
    half_rows = PLANE // 2 * MAIN_ROWS + BAND_ROWS
    return pl.pallas_call(
        functools.partial(main_kernel, steps=steps, planes=PLANES // steps),
        grid=(steps,),
        in_specs=[
            pl.BlockSpec((block, span), lambda s: (s, 0)),
            pl.BlockSpec((words.shape[0], block), lambda s: (0, s)),
            pl.BlockSpec((ranks, block), lambda s: (0, s)),
            pl.BlockSpec((ranks, span), lambda s: (0, 0)),
        ],
        out_specs=[
            pl.BlockSpec((half_rows, 128), lambda s: (0, 0)),
            pl.BlockSpec((half_rows, 128), lambda s: (0, 0)),
            pl.BlockSpec((2, 2, BAND, span), lambda s: (0, 0, 0, 0)),
            pl.BlockSpec((2, 2, BAND, span), lambda s: (0, 0, 0, 0)),
        ],
        scratch_shapes=[pltpu.VMEM((ranks, span), jnp.float32)],
        out_shape=[
            jax.ShapeDtypeStruct((half_rows, 128), jnp.float32),
            jax.ShapeDtypeStruct((half_rows, 128), jnp.float32),
            jax.ShapeDtypeStruct((2, 2, BAND, span), jnp.float32),
            jax.ShapeDtypeStruct((2, 2, BAND, span), jnp.float32),
        ],
        cost_estimate=pl.CostEstimate(flops=805306368, bytes_accessed=6_000_000, transcendentals=0),
        compiler_params=pltpu.CompilerParams(vmem_limit_bytes=24 << 20),
        name="main_terms",
    )(*(pltpu.with_memory_space_constraint(a, pltpu.HBM) for a in (observed, words, factor, time)))


def pair_kernel(keep, got, out):
    first = lax.axis_index("core") == 0
    tail = PLANE // 2 * MAIN_ROWS
    mine, other = keep[tail:], got[tail:]
    for x in range(PLANE // 2):
        at = slice(x * MAIN_ROWS, (x + 1) * MAIN_ROWS)
        out[x, :MAIN_ROWS] = keep[at] + got[at]
        out[x, MAIN_ROWS : MAIN_ROWS + BAND_ROWS] = jnp.where(first, mine, other)
        out[x, MAIN_ROWS + BAND_ROWS :] = jnp.where(first, other, mine)


def pair_terms(keep, got):
    in_vmem = pl.BlockSpec(memory_space=pltpu.VMEM)
    return pl.pallas_call(
        pair_kernel,
        in_specs=[in_vmem, in_vmem],
        out_specs=in_vmem,
        out_shape=jax.ShapeDtypeStruct((PLANE // 2, ROWS, 128), jnp.float32),
        cost_estimate=pl.CostEstimate(flops=100_000, bytes_accessed=1_400_000, transcendentals=0),
        compiler_params=pltpu.CompilerParams(vmem_limit_bytes=8 << 20),
        name="pair_terms",
    )(keep, got)


def split_kernel(got, planes, passed):
    total = got[0, :MAIN_ROWS]
    for x in range(1, PLANE // 2):
        total = total + got[x, :MAIN_ROWS]
    half = SHARE // 2
    for z in range(PLANES):
        planes[z] = total[half * z : half * z + half]
    late = place_of(AXES[3:]) < PLANE // 2
    for span in range(HOPS):
        ends = []
        for source in (PLANE - HOPS + span, span):
            at = MAIN_ROWS + BAND_ROWS * (source & 1)
            ends.append(got[source >> 1, at : at + BAND_ROWS])
        passed[span] = jnp.where(late, ends[0], ends[1])


def split_terms(got):
    in_vmem = pl.BlockSpec(memory_space=pltpu.VMEM)
    return pl.pallas_call(
        split_kernel,
        in_specs=[in_vmem],
        out_specs=[in_vmem, in_vmem],
        out_shape=[
            jax.ShapeDtypeStruct((PLANES, SHARE // 2, 128), jnp.float32),
            jax.ShapeDtypeStruct((HOPS, BAND_ROWS, 128), jnp.float32),
        ],
        cost_estimate=pl.CostEstimate(flops=100_000, bytes_accessed=700_000, transcendentals=0),
        compiler_params=pltpu.CompilerParams(vmem_limit_bytes=8 << 20),
        name="split_terms",
    )(got)


def shifted_tiles(start, count, read):
    first, lane = start >> 7, start & 127
    back = (128 - lane) & 127
    rolled = [pltpu.roll(read(first + i), back, 1) for i in range(count + 1)]
    inside = lax.broadcasted_iota(jnp.int32, (BAND, 128), 1) < 128 - lane
    return [jnp.where(inside, rolled[i], rolled[i + 1]) for i in range(count)]


def ar_kernel(lags, weights, plane, beside, home, out, spans, errors, weight_rows):
    edge = HOPS * TILES
    for span in range(HOPS):
        for tile in range(TILES):
            value = beside[span, BAND * tile : BAND * tile + BAND]
            spans[span * TILES + tile] = value
            spans[edge + PLANE * TILES + span * TILES + tile] = value
    for span in range(PLANE):
        for tile in range(TILES):
            spans[edge + span * TILES + tile] = plane[span, BAND * tile : BAND * tile + BAND]
    weight_rows[...] = weights[...].T
    mine = weight_rows[pl.ds(pl.multiple_of(place_of(FEEDER_AXES) * BAND, BAND), BAND), :]
    own_tile = edge + place_of(AXES[3:]) * TILES
    own_column = own_tile * 128
    count = lags.shape[0]
    gains = [jnp.broadcast_to(mine[:, k : k + 1], (BAND, 128)) for k in range(count)]
    parts = [jnp.zeros((BAND, 128), jnp.float32) for _ in range(CHUNKS)]
    for k in range(count):
        moved = shifted_tiles(own_column - lags[k], CHUNKS, lambda i: spans[i])
        parts = [part + gains[k] * tile for part, tile in zip(parts, moved)]
    lane = lax.broadcasted_iota(jnp.int32, (BAND, 128), 1)
    first = place_of(TM_AXES) * SPAN
    for chunk in range(CHUNKS):
        column = first + 128 * chunk + lane
        inside = (column >= LAGMAX) & (column < TM * SPAN)
        errors[chunk] = jnp.where(inside, spans[own_tile + chunk] - parts[chunk], 0.0)
    errors[CHUNKS] = jnp.zeros((BAND, 128), jnp.float32)
    carried = [jnp.zeros((BAND, 128), jnp.float32) for _ in range(TILES)]
    for k in range(count):
        moved = shifted_tiles(lags[k], TILES, lambda i: errors[i])
        carried = [part + gains[k] * tile for part, tile in zip(carried, moved)]
    for tile in range(TILES):
        at = slice(128 * tile, 128 * tile + 128)
        out[:, at] = (
            home[:, at]
            + LAM_AR * (errors[tile] - carried[tile])
            + LAM_X * spans[own_tile + tile]
        )


def ar_terms(lags, weights, plane, beside, home):
    in_vmem = pl.BlockSpec(memory_space=pltpu.VMEM)
    in_smem = pl.BlockSpec(memory_space=pltpu.SMEM)
    tiles = (2 * HOPS + PLANE) * TILES
    return pl.pallas_call(
        ar_kernel,
        in_specs=[in_smem] + [in_vmem] * 4,
        out_specs=in_vmem,
        out_shape=jax.ShapeDtypeStruct((BAND, SPAN), jnp.float32),
        scratch_shapes=[
            pltpu.VMEM((tiles + 1, BAND, 128), jnp.float32),
            pltpu.VMEM((CHUNKS + 1, BAND, 128), jnp.float32),
            pltpu.VMEM(weights.shape[::-1], jnp.float32),
        ],
        cost_estimate=pl.CostEstimate(flops=2_000_000, bytes_accessed=400_000, transcendentals=0),
        compiler_params=pltpu.CompilerParams(vmem_limit_bytes=8 << 20),
        name="ar_terms",
    )(lags, weights, plane, beside, home)


def per_device(
    observed, mask_words, feeder_factor, time_factor, ar_weight, lags, moment_first, moment_second
):
    ranks = time_factor.shape[0]
    tm_place = lax.axis_index(TM_AXES)

    keep, send, bands, sent_bands = main_terms(observed, mask_words.T, feeder_factor.T, time_factor)
    got = lax.ppermute(send, "core", [(0, 1), (1, 0)])
    own_factor = lax.dynamic_slice_in_dim(feeder_factor, tm_place * SHARE, SHARE, 0)
    bands = bands + lax.ppermute(sent_bands, "y", [(0, 1), (1, 0), (2, 3), (3, 2)])
    pair = pair_terms(keep, got)
    bands = bands[0] + lax.ppermute(bands[1], "y", [(0, 3), (3, 0), (1, 2), (2, 1)])
    got = lax.all_to_all(pair, "x", 0, 0, tiled=True)
    away = lax.ppermute(bands[1], "z_hi", [(0, 1), (1, 0)])

    planes, passed = split_terms(got)
    plane = got[:, MAIN_ROWS:].reshape(PLANE, BAND_ROWS, 128)
    pairs = [(t, t + PLANE) for t in range(TM - PLANE) if t % PLANE < PLANE // 2]
    pairs += [(t, t - PLANE) for t in range(PLANE, TM) if t % PLANE >= PLANE // 2]
    beside = lax.ppermute(passed, TM_AXES, pairs)
    share = lax.all_to_all(planes, "z_lo", 0, 0, tiled=True)
    share = share.sum(0)
    time_grad = ar_terms(lags, ar_weight, plane, beside, bands[0]) + away

    grad_share = jnp.concatenate([share[:, :ranks], share[:, ranks:]], axis=0)
    factor_grad = grad_share + LAM_F * own_factor
    new_first = BETA_ONE * moment_first + (1.0 - BETA_ONE) * factor_grad
    new_second = BETA_TWO * moment_second + (1.0 - BETA_TWO) * factor_grad * factor_grad
    update = (
        LEARNING_RATE * (new_first / BIAS_FIRST) / (jnp.sqrt(new_second / BIAS_SECOND) + ADAM_EPS)
    )
    return (own_factor - update, new_first, new_second, time_grad)


def solution(mesh):
    fine = Mesh(mesh.devices.reshape(2, 4, 8, 4, 2), AXES)
    rows = P(AXES, None)
    placed = (
        P(FEEDER_AXES, TM_AXES),
        P(FEEDER_AXES, TM_AXES),
        P(FEEDER_AXES, None),
        P(None, TM_AXES),
        P(),
        P(),
        rows,
        rows,
    )
    return jax.shard_map(
        per_device,
        mesh=fine,
        in_specs=placed,
        out_specs=(rows, rows, rows, P(FEEDER_AXES, TM_AXES)),
        check_vma=False,
    )
```

```python
import functools

import jax
import jax.numpy as jnp
from jax import lax
from jax.experimental import pallas as pl
from jax.experimental.pallas import tpu as pltpu
from jax.sharding import Mesh
from jax.sharding import PartitionSpec as P

LAGMAX = 1440
DATA_WEIGHT = 1.0 / 64.0
LAM_F = 0.1
LAM_X = 0.01
LAM_AR = 8.0
BETA_ONE = 0.9
BETA_TWO = 0.999
BIAS_FIRST = 1.0 - 0.9**8
BIAS_SECOND = 1.0 - 0.999**8
LEARNING_RATE = 0.05
ADAM_EPS = 1e-08

AXES = ("z_hi", "y", "z_lo", "x", "core")
FEEDER_AXES, TM_AXES = AXES[:2], AXES[2:]
PLANES, PLANE = 8, 8
TM = PLANES * PLANE
SHARE = 48
BAND = 8
SPAN = 512
TILES = SPAN // 128
MAIN_ROWS = PLANES * SHARE // 2
BAND_ROWS = BAND * TILES
HOPS = 3
CHUNKS = (HOPS + 1) * TILES


def gray(place):
    return place ^ (place >> 1)


def place_of(axes):
    place = 0
    for axis in axes:
        place = place * lax.axis_size(axis) + lax.axis_index(axis)
    return place


def main_kernel(
    observed, words, factor, time, keep, send, own_band, time_keep, time_send, total, *, steps, planes
):
    step = pl.program_id(0)
    factor_half = factor[...].astype(jnp.bfloat16)
    time_half = time[...].astype(jnp.bfloat16)
    predicted = lax.dot_general(
        factor_half, time_half, (((0,), (0,)), ((), ())), preferred_element_type=jnp.float32
    )
    word_count, span = words.shape[0], time.shape[1]
    spread = (
        lax.broadcasted_iota(jnp.int32, (word_count, span), 1) >> 3
        == lax.broadcasted_iota(jnp.int32, (word_count, span), 0)
    )
    power = 1.0 / jnp.left_shift(2, lax.broadcasted_iota(jnp.int32, (1, span), 1) & 7).astype(jnp.float32)
    spread = jnp.where(spread, power, 0.0).astype(jnp.bfloat16)
    wide = lax.dot_general(
        words[...].astype(jnp.float32).astype(jnp.bfloat16),
        spread,
        (((0,), (0,)), ((), ())),
        preferred_element_type=jnp.float32,
    )
    residual = jnp.where(
        wide - jnp.floor(wide) >= 0.5, predicted - observed[...].astype(jnp.float32), 0.0
    ).astype(jnp.bfloat16)
    rows = DATA_WEIGHT * lax.dot_general(
        residual, time_half, (((1,), (1,)), ((), ())), preferred_element_type=jnp.float32
    )
    half = SHARE // 2
    first = lax.axis_index("core") == 0
    for plane in range(planes):
        for x in range(PLANE // 2):
            pair = []
            for core in range(2):
                start = (plane * PLANE + 2 * x + core) * SHARE
                pair.append(
                    jnp.concatenate(
                        [rows[start : start + half], rows[start + half : start + SHARE]], axis=1
                    )
                )
            at = pl.ds(pl.multiple_of(x * MAIN_ROWS + (step * planes + plane) * half, 8), half)
            keep[at] = jnp.where(first, pair[0], pair[1])
            send[at] = jnp.where(first, pair[1], pair[0])
    term = jnp.dot(factor_half, residual, preferred_element_type=jnp.float32)

    @pl.when(step == 0)
    def _():
        total[...] = term
        own = time[pl.ds(pl.multiple_of(place_of(FEEDER_AXES) * BAND, BAND), BAND), :]
        for tile in range(TILES):
            at = PLANE // 2 * MAIN_ROWS + BAND * tile
            send[at : at + BAND] = own[:, 128 * tile : 128 * tile + 128]
            own_band[BAND * tile : BAND * tile + BAND] = own[:, 128 * tile : 128 * tile + 128]

    @pl.when(step > 0)
    def _():
        total[...] = total[...] + term

    @pl.when(step == steps - 1)
    def _():
        z_hi, y_ring = lax.axis_index("z_hi"), gray(lax.axis_index("y"))
        for near in range(4):
            far = near ^ y_ring
            for z in range(2):
                band = (z ^ z_hi) * 4 + (far ^ (far >> 1))
                rows_out = DATA_WEIGHT * total[pl.ds(pl.multiple_of(band * BAND, BAND), BAND), :]
                if near & 1:
                    time_send[near >> 1, z] = rows_out
                else:
                    time_keep[near >> 1, z] = rows_out


def main_terms(observed, words, factor, time, steps=4):
    feeders, span = observed.shape
    ranks, block = factor.shape[0], feeders // steps
    half_rows = PLANE // 2 * MAIN_ROWS
    return pl.pallas_call(
        functools.partial(main_kernel, steps=steps, planes=PLANES // steps),
        grid=(steps,),
        in_specs=[
            pl.BlockSpec((block, span), lambda s: (s, 0)),
            pl.BlockSpec((words.shape[0], block), lambda s: (0, s)),
            pl.BlockSpec((ranks, block), lambda s: (0, s)),
            pl.BlockSpec((ranks, span), lambda s: (0, 0)),
        ],
        out_specs=[
            pl.BlockSpec((half_rows, 128), lambda s: (0, 0)),
            pl.BlockSpec((half_rows + BAND_ROWS, 128), lambda s: (0, 0)),
            pl.BlockSpec((BAND_ROWS, 128), lambda s: (0, 0)),
            pl.BlockSpec((2, 2, BAND, span), lambda s: (0, 0, 0, 0)),
            pl.BlockSpec((2, 2, BAND, span), lambda s: (0, 0, 0, 0)),
        ],
        scratch_shapes=[pltpu.VMEM((ranks, span), jnp.float32)],
        out_shape=[
            jax.ShapeDtypeStruct((half_rows, 128), jnp.float32),
            jax.ShapeDtypeStruct((half_rows + BAND_ROWS, 128), jnp.float32),
            jax.ShapeDtypeStruct((BAND_ROWS, 128), jnp.float32),
            jax.ShapeDtypeStruct((2, 2, BAND, span), jnp.float32),
            jax.ShapeDtypeStruct((2, 2, BAND, span), jnp.float32),
        ],
        cost_estimate=pl.CostEstimate(flops=805306368, bytes_accessed=6_000_000, transcendentals=0),
        compiler_params=pltpu.CompilerParams(vmem_limit_bytes=24 << 20),
        name="main_terms",
    )(*(pltpu.with_memory_space_constraint(a, pltpu.HBM) for a in (observed, words, factor, time)))


def pair_kernel(keep, own_band, got, out, both):
    first = lax.axis_index("core") == 0
    mine, other = own_band[...], got[PLANE // 2 * MAIN_ROWS :]
    both[0] = jnp.where(first, mine, other)
    both[1] = jnp.where(first, other, mine)
    for x in range(PLANE // 2):
        at = slice(x * MAIN_ROWS, (x + 1) * MAIN_ROWS)
        out[x] = keep[at] + got[at]


def sum_kernel(got, planes):
    total = got[0]
    for x in range(1, PLANE // 2):
        total = total + got[x]
    half = SHARE // 2
    for z in range(PLANES):
        planes[z] = total[half * z : half * z + half]


def on_chip(kernel, args, outs):
    in_vmem = pl.BlockSpec(memory_space=pltpu.VMEM)
    return pl.pallas_call(
        kernel,
        in_specs=[in_vmem] * len(args),
        out_specs=[in_vmem] * len(outs),
        out_shape=[jax.ShapeDtypeStruct(shape, jnp.float32) for shape in outs],
        cost_estimate=pl.CostEstimate(flops=100_000, bytes_accessed=1_000_000, transcendentals=0),
        compiler_params=pltpu.CompilerParams(vmem_limit_bytes=8 << 20),
    )(*args)


def shifted_tiles(start, count, read):
    first, lane = start >> 7, start & 127
    back = (128 - lane) & 127
    rolled = [pltpu.roll(read(first + i), back, 1) for i in range(count + 1)]
    inside = lax.broadcasted_iota(jnp.int32, (BAND, 128), 1) < 128 - lane
    return [jnp.where(inside, rolled[i], rolled[i + 1]) for i in range(count)]


def ar_kernel(lags, weights, before, both, after, far, home, out, spans, errors, weight_rows):
    for tile in range(TILES):
        at = slice(BAND * tile, BAND * tile + BAND)
        spans[tile] = far[at]
        spans[7 * TILES + tile] = far[at]
        for core in range(2):
            for pair, source in enumerate((before, both, after)):
                spans[(1 + 2 * pair + core) * TILES + tile] = source[core, at]
    weight_rows[...] = weights[...].T
    mine = weight_rows[pl.ds(pl.multiple_of(place_of(FEEDER_AXES) * BAND, BAND), BAND), :]
    own_tile = (HOPS + lax.axis_index("core")) * TILES
    own_column = own_tile * 128
    count = lags.shape[0]
    gains = [jnp.broadcast_to(mine[:, k : k + 1], (BAND, 128)) for k in range(count)]
    parts = [jnp.zeros((BAND, 128), jnp.float32) for _ in range(CHUNKS)]
    for k in range(count):
        moved = shifted_tiles(own_column - lags[k], CHUNKS, lambda i: spans[i])
        parts = [part + gains[k] * tile for part, tile in zip(parts, moved)]
    lane = lax.broadcasted_iota(jnp.int32, (BAND, 128), 1)
    first = place_of(TM_AXES) * SPAN
    for chunk in range(CHUNKS):
        column = first + 128 * chunk + lane
        inside = (column >= LAGMAX) & (column < TM * SPAN)
        errors[chunk] = jnp.where(inside, spans[own_tile + chunk] - parts[chunk], 0.0)
    errors[CHUNKS] = jnp.zeros((BAND, 128), jnp.float32)
    carried = [jnp.zeros((BAND, 128), jnp.float32) for _ in range(TILES)]
    for k in range(count):
        moved = shifted_tiles(lags[k], TILES, lambda i: errors[i])
        carried = [part + gains[k] * tile for part, tile in zip(carried, moved)]
    for tile in range(TILES):
        at = slice(128 * tile, 128 * tile + 128)
        out[:, at] = (
            home[:, at]
            + LAM_AR * (errors[tile] - carried[tile])
            + LAM_X * spans[own_tile + tile]
        )


def ar_terms(lags, weights, before, both, after, far, home):
    in_vmem = pl.BlockSpec(memory_space=pltpu.VMEM)
    in_smem = pl.BlockSpec(memory_space=pltpu.SMEM)
    return pl.pallas_call(
        ar_kernel,
        in_specs=[in_smem] + [in_vmem] * 6,
        out_specs=in_vmem,
        out_shape=jax.ShapeDtypeStruct((BAND, SPAN), jnp.float32),
        scratch_shapes=[
            pltpu.VMEM((2 * (HOPS + 1) * TILES + 1, BAND, 128), jnp.float32),
            pltpu.VMEM((CHUNKS + 1, BAND, 128), jnp.float32),
            pltpu.VMEM(weights.shape[::-1], jnp.float32),
        ],
        cost_estimate=pl.CostEstimate(flops=2_000_000, bytes_accessed=400_000, transcendentals=0),
        compiler_params=pltpu.CompilerParams(vmem_limit_bytes=8 << 20),
        name="ar_terms",
    )(lags, weights, before, both, after, far, home)


def per_device(
    observed, mask_words, feeder_factor, time_factor, ar_weight, lags, moment_first, moment_second
):
    ranks = time_factor.shape[0]
    tm_place = lax.axis_index(TM_AXES)

    keep, send, own_band, bands, sent_bands = main_terms(
        observed, mask_words.T, feeder_factor.T, time_factor
    )
    got = lax.ppermute(send, "core", [(0, 1), (1, 0)])
    own_factor = lax.dynamic_slice_in_dim(feeder_factor, tm_place * SHARE, SHARE, 0)
    bands = bands + lax.ppermute(sent_bands, "y", [(0, 1), (1, 0), (2, 3), (3, 2)])
    pair, both = on_chip(
        pair_kernel, (keep, own_band, got), ((PLANE // 2, MAIN_ROWS, 128), (2, BAND_ROWS, 128))
    )
    bands = bands[0] + lax.ppermute(bands[1], "y", [(0, 3), (3, 0), (1, 2), (2, 1)])
    got = lax.all_to_all(pair, "x", 0, 0, tiled=True)
    away = lax.ppermute(bands[1], "z_hi", [(0, 1), (1, 0)])

    before = lax.ppermute(both, TM_AXES, [(t, t + 2) for t in range(TM - 2)])
    after = lax.ppermute(both, TM_AXES, [(t, t - 2) for t in range(2, TM)])
    pairs = [(t, t + 3 if t % 2 else t - 3) for t in range(TM)]
    far = lax.ppermute(own_band, TM_AXES, [(t, to) for t, to in pairs if 0 <= to < TM])
    (planes,) = on_chip(sum_kernel, (got,), ((PLANES, SHARE // 2, 128),))
    share = lax.all_to_all(planes, "z_lo", 0, 0, tiled=True)
    share = share.sum(0)
    half_grad = ar_terms(lags, ar_weight, before, both, after, far, bands[0])
    time_grad = half_grad + away

    grad_share = jnp.concatenate([share[:, :ranks], share[:, ranks:]], axis=0)
    factor_grad = grad_share + LAM_F * own_factor
    new_first = BETA_ONE * moment_first + (1.0 - BETA_ONE) * factor_grad
    new_second = BETA_TWO * moment_second + (1.0 - BETA_TWO) * factor_grad * factor_grad
    update = (
        LEARNING_RATE * (new_first / BIAS_FIRST) / (jnp.sqrt(new_second / BIAS_SECOND) + ADAM_EPS)
    )
    return (own_factor - update, new_first, new_second, time_grad)


def solution(mesh):
    fine = Mesh(mesh.devices.reshape(2, 4, 8, 4, 2), AXES)
    rows = P(AXES, None)
    placed = (
        P(FEEDER_AXES, TM_AXES),
        P(FEEDER_AXES, TM_AXES),
        P(FEEDER_AXES, None),
        P(None, TM_AXES),
        P(),
        P(),
        rows,
        rows,
    )
    return jax.shard_map(
        per_device,
        mesh=fine,
        in_specs=placed,
        out_specs=(rows, rows, rows, P(FEEDER_AXES, TM_AXES)),
        check_vma=False,
    )
```

```python
import functools

import jax
import jax.numpy as jnp
from jax import lax
from jax.experimental import pallas as pl
from jax.experimental.pallas import tpu as pltpu
from jax.sharding import Mesh
from jax.sharding import PartitionSpec as P

LAGMAX = 1440
DATA_WEIGHT = 1.0 / 64.0
LAM_F = 0.1
LAM_X = 0.01
LAM_AR = 8.0
BETA_ONE = 0.9
BETA_TWO = 0.999
BIAS_FIRST = 1.0 - 0.9**8
BIAS_SECOND = 1.0 - 0.999**8
LEARNING_RATE = 0.05
ADAM_EPS = 1e-08

AXES = ("z_hi", "y", "z_lo", "x", "core")
FEEDER_AXES, TM_AXES = AXES[:2], AXES[2:]
PLANES, PLANE = 8, 8
TM = PLANES * PLANE
SHARE = 48
BAND = 8
SPAN = 512
TILES = SPAN // 128
MAIN_ROWS = PLANES * SHARE // 2
BAND_ROWS = BAND * TILES
ROWS = MAIN_ROWS + 2 * BAND_ROWS
HOPS = 3
CHUNKS = (HOPS + 1) * TILES


def gray(place):
    return place ^ (place >> 1)


def place_of(axes):
    place = 0
    for axis in axes:
        place = place * lax.axis_size(axis) + lax.axis_index(axis)
    return place


def main_kernel(
    observed, words, factor, time, keep, send, time_keep, time_send, total, *, steps, planes
):
    step = pl.program_id(0)
    factor_half = factor[...].astype(jnp.bfloat16)
    time_half = time[...].astype(jnp.bfloat16)
    predicted = lax.dot_general(
        factor_half, time_half, (((0,), (0,)), ((), ())), preferred_element_type=jnp.float32
    )
    word_count, span = words.shape[0], time.shape[1]
    spread = (
        lax.broadcasted_iota(jnp.int32, (word_count, span), 1) >> 3
        == lax.broadcasted_iota(jnp.int32, (word_count, span), 0)
    )
    power = 1.0 / jnp.left_shift(2, lax.broadcasted_iota(jnp.int32, (1, span), 1) & 7).astype(jnp.float32)
    spread = jnp.where(spread, power, 0.0).astype(jnp.bfloat16)
    wide = lax.dot_general(
        words[...].astype(jnp.float32).astype(jnp.bfloat16),
        spread,
        (((0,), (0,)), ((), ())),
        preferred_element_type=jnp.float32,
    )
    residual = jnp.where(
        wide - jnp.floor(wide) >= 0.5, predicted - observed[...].astype(jnp.float32), 0.0
    ).astype(jnp.bfloat16)
    rows = DATA_WEIGHT * lax.dot_general(
        residual, time_half, (((1,), (1,)), ((), ())), preferred_element_type=jnp.float32
    )
    half = SHARE // 2
    first = lax.axis_index("core") == 0
    for plane in range(planes):
        for x in range(PLANE // 2):
            pair = []
            for core in range(2):
                start = (plane * PLANE + 2 * x + core) * SHARE
                pair.append(
                    jnp.concatenate(
                        [rows[start : start + half], rows[start + half : start + SHARE]], axis=1
                    )
                )
            at = pl.ds(pl.multiple_of(x * MAIN_ROWS + (step * planes + plane) * half, 8), half)
            keep[at] = jnp.where(first, pair[0], pair[1])
            send[at] = jnp.where(first, pair[1], pair[0])
    term = jnp.dot(factor_half, residual, preferred_element_type=jnp.float32)

    @pl.when(step == 0)
    def _():
        total[...] = term
        own = time[pl.ds(pl.multiple_of(place_of(FEEDER_AXES) * BAND, BAND), BAND), :]
        for tile in range(TILES):
            at = PLANE // 2 * MAIN_ROWS + BAND * tile
            keep[at : at + BAND] = own[:, 128 * tile : 128 * tile + 128]
            send[at : at + BAND] = own[:, 128 * tile : 128 * tile + 128]

    @pl.when(step > 0)
    def _():
        total[...] = total[...] + term

    @pl.when(step == steps - 1)
    def _():
        z_hi, y_ring = lax.axis_index("z_hi"), gray(lax.axis_index("y"))
        for near in range(4):
            far = near ^ y_ring
            for z in range(2):
                band = (z ^ z_hi) * 4 + (far ^ (far >> 1))
                rows_out = DATA_WEIGHT * total[pl.ds(pl.multiple_of(band * BAND, BAND), BAND), :]
                if near & 1:
                    time_send[near >> 1, z] = rows_out
                else:
                    time_keep[near >> 1, z] = rows_out


def main_terms(observed, words, factor, time, steps=2):
    feeders, span = observed.shape
    ranks, block = factor.shape[0], feeders // steps
    half_rows = PLANE // 2 * MAIN_ROWS + BAND_ROWS
    return pl.pallas_call(
        functools.partial(main_kernel, steps=steps, planes=PLANES // steps),
        grid=(steps,),
        in_specs=[
            pl.BlockSpec((block, span), lambda s: (s, 0)),
            pl.BlockSpec((words.shape[0], block), lambda s: (0, s)),
            pl.BlockSpec((ranks, block), lambda s: (0, s)),
            pl.BlockSpec((ranks, span), lambda s: (0, 0)),
        ],
        out_specs=[
            pl.BlockSpec((half_rows, 128), lambda s: (0, 0)),
            pl.BlockSpec((half_rows, 128), lambda s: (0, 0)),
            pl.BlockSpec((2, 2, BAND, span), lambda s: (0, 0, 0, 0)),
            pl.BlockSpec((2, 2, BAND, span), lambda s: (0, 0, 0, 0)),
        ],
        scratch_shapes=[pltpu.VMEM((ranks, span), jnp.float32)],
        out_shape=[
            jax.ShapeDtypeStruct((half_rows, 128), jnp.float32),
            jax.ShapeDtypeStruct((half_rows, 128), jnp.float32),
            jax.ShapeDtypeStruct((2, 2, BAND, span), jnp.float32),
            jax.ShapeDtypeStruct((2, 2, BAND, span), jnp.float32),
        ],
        cost_estimate=pl.CostEstimate(flops=805306368, bytes_accessed=6_000_000, transcendentals=0),
        compiler_params=pltpu.CompilerParams(vmem_limit_bytes=24 << 20),
        name="main_terms",
    )(*(pltpu.with_memory_space_constraint(a, pltpu.HBM) for a in (observed, words, factor, time)))


def pair_kernel(keep, got, out):
    first = lax.axis_index("core") == 0
    tail = PLANE // 2 * MAIN_ROWS
    mine, other = keep[tail:], got[tail:]
    for x in range(PLANE // 2):
        at = slice(x * MAIN_ROWS, (x + 1) * MAIN_ROWS)
        out[x, :MAIN_ROWS] = keep[at] + got[at]
        out[x, MAIN_ROWS : MAIN_ROWS + BAND_ROWS] = jnp.where(first, mine, other)
        out[x, MAIN_ROWS + BAND_ROWS :] = jnp.where(first, other, mine)


def pair_terms(keep, got):
    in_vmem = pl.BlockSpec(memory_space=pltpu.VMEM)
    return pl.pallas_call(
        pair_kernel,
        in_specs=[in_vmem, in_vmem],
        out_specs=in_vmem,
        out_shape=jax.ShapeDtypeStruct((PLANE // 2, ROWS, 128), jnp.float32),
        cost_estimate=pl.CostEstimate(flops=100_000, bytes_accessed=1_400_000, transcendentals=0),
        compiler_params=pltpu.CompilerParams(vmem_limit_bytes=8 << 20),
        name="pair_terms",
    )(keep, got)


def split_kernel(got, planes, passed):
    total = got[0, :MAIN_ROWS]
    for x in range(1, PLANE // 2):
        total = total + got[x, :MAIN_ROWS]
    half = SHARE // 2
    for z in range(PLANES):
        planes[z] = total[half * z : half * z + half]
    late = place_of(AXES[3:]) < PLANE // 2
    for span in range(HOPS):
        ends = []
        for source in (PLANE - HOPS + span, span):
            at = MAIN_ROWS + BAND_ROWS * (source & 1)
            ends.append(got[source >> 1, at : at + BAND_ROWS])
        passed[span] = jnp.where(late, ends[0], ends[1])


def split_terms(got):
    in_vmem = pl.BlockSpec(memory_space=pltpu.VMEM)
    return pl.pallas_call(
        split_kernel,
        in_specs=[in_vmem],
        out_specs=[in_vmem, in_vmem],
        out_shape=[
            jax.ShapeDtypeStruct((PLANES, SHARE // 2, 128), jnp.float32),
            jax.ShapeDtypeStruct((HOPS, BAND_ROWS, 128), jnp.float32),
        ],
        cost_estimate=pl.CostEstimate(flops=100_000, bytes_accessed=700_000, transcendentals=0),
        compiler_params=pltpu.CompilerParams(vmem_limit_bytes=8 << 20),
        name="split_terms",
    )(got)


def shifted_tiles(start, count, read):
    first, lane = start >> 7, start & 127
    back = (128 - lane) & 127
    rolled = [pltpu.roll(read(first + i), back, 1) for i in range(count + 1)]
    inside = lax.broadcasted_iota(jnp.int32, (BAND, 128), 1) < 128 - lane
    return [jnp.where(inside, rolled[i], rolled[i + 1]) for i in range(count)]


def ar_kernel(lags, weights, plane, beside, home, out, spans, errors, weight_rows):
    edge = HOPS * TILES
    for span in range(HOPS):
        for tile in range(TILES):
            value = beside[span, BAND * tile : BAND * tile + BAND]
            spans[span * TILES + tile] = value
            spans[edge + PLANE * TILES + span * TILES + tile] = value
    for span in range(PLANE):
        for tile in range(TILES):
            spans[edge + span * TILES + tile] = plane[span, BAND * tile : BAND * tile + BAND]
    weight_rows[...] = weights[...].T
    mine = weight_rows[pl.ds(pl.multiple_of(place_of(FEEDER_AXES) * BAND, BAND), BAND), :]
    own_tile = edge + place_of(AXES[3:]) * TILES
    own_column = own_tile * 128
    count = lags.shape[0]
    gains = [jnp.broadcast_to(mine[:, k : k + 1], (BAND, 128)) for k in range(count)]
    parts = [jnp.zeros((BAND, 128), jnp.float32) for _ in range(CHUNKS)]
    for k in range(count):
        moved = shifted_tiles(own_column - lags[k], CHUNKS, lambda i: spans[i])
        parts = [part + gains[k] * tile for part, tile in zip(parts, moved)]
    lane = lax.broadcasted_iota(jnp.int32, (BAND, 128), 1)
    first = place_of(TM_AXES) * SPAN
    for chunk in range(CHUNKS):
        column = first + 128 * chunk + lane
        inside = (column >= LAGMAX) & (column < TM * SPAN)
        errors[chunk] = jnp.where(inside, spans[own_tile + chunk] - parts[chunk], 0.0)
    errors[CHUNKS] = jnp.zeros((BAND, 128), jnp.float32)
    carried = [jnp.zeros((BAND, 128), jnp.float32) for _ in range(TILES)]
    for k in range(count):
        moved = shifted_tiles(lags[k], TILES, lambda i: errors[i])
        carried = [part + gains[k] * tile for part, tile in zip(carried, moved)]
    for tile in range(TILES):
        at = slice(128 * tile, 128 * tile + 128)
        out[:, at] = (
            home[:, at]
            + LAM_AR * (errors[tile] - carried[tile])
            + LAM_X * spans[own_tile + tile]
        )


def ar_terms(lags, weights, plane, beside, home):
    in_vmem = pl.BlockSpec(memory_space=pltpu.VMEM)
    in_smem = pl.BlockSpec(memory_space=pltpu.SMEM)
    tiles = (2 * HOPS + PLANE) * TILES
    return pl.pallas_call(
        ar_kernel,
        in_specs=[in_smem] + [in_vmem] * 4,
        out_specs=in_vmem,
        out_shape=jax.ShapeDtypeStruct((BAND, SPAN), jnp.float32),
        scratch_shapes=[
            pltpu.VMEM((tiles + 1, BAND, 128), jnp.float32),
            pltpu.VMEM((CHUNKS + 1, BAND, 128), jnp.float32),
            pltpu.VMEM(weights.shape[::-1], jnp.float32),
        ],
        cost_estimate=pl.CostEstimate(flops=2_000_000, bytes_accessed=400_000, transcendentals=0),
        compiler_params=pltpu.CompilerParams(vmem_limit_bytes=8 << 20),
        name="ar_terms",
    )(lags, weights, plane, beside, home)


def per_device(
    observed, mask_words, feeder_factor, time_factor, ar_weight, lags, moment_first, moment_second
):
    ranks = time_factor.shape[0]
    tm_place = lax.axis_index(TM_AXES)

    keep, send, bands, sent_bands = main_terms(observed, mask_words.T, feeder_factor.T, time_factor)
    got = lax.ppermute(send, "core", [(0, 1), (1, 0)])
    own_factor = lax.dynamic_slice_in_dim(feeder_factor, tm_place * SHARE, SHARE, 0)
    bands = bands + lax.ppermute(sent_bands, "y", [(0, 1), (1, 0), (2, 3), (3, 2)])
    pair = pair_terms(keep, got)
    bands = bands[0] + lax.ppermute(bands[1], "y", [(0, 3), (3, 0), (1, 2), (2, 1)])
    got = lax.all_to_all(pair, "x", 0, 0, tiled=True)
    away = lax.ppermute(bands[1], "z_hi", [(0, 1), (1, 0)])

    planes, passed = split_terms(got)
    plane = got[:, MAIN_ROWS:].reshape(PLANE, BAND_ROWS, 128)
    pairs = [(t, t + PLANE) for t in range(TM - PLANE) if t % PLANE < PLANE // 2]
    pairs += [(t, t - PLANE) for t in range(PLANE, TM) if t % PLANE >= PLANE // 2]
    beside = lax.ppermute(passed, TM_AXES, pairs)
    share = lax.all_to_all(planes, "z_lo", 0, 0, tiled=True)
    share = share.sum(0)
    half_grad = ar_terms(lags, ar_weight, plane, beside, bands[0])
    time_grad = half_grad + away

    grad_share = jnp.concatenate([share[:, :ranks], share[:, ranks:]], axis=0)
    factor_grad = grad_share + LAM_F * own_factor
    new_first = BETA_ONE * moment_first + (1.0 - BETA_ONE) * factor_grad
    new_second = BETA_TWO * moment_second + (1.0 - BETA_TWO) * factor_grad * factor_grad
    update = (
        LEARNING_RATE * (new_first / BIAS_FIRST) / (jnp.sqrt(new_second / BIAS_SECOND) + ADAM_EPS)
    )
    new_factor = own_factor - update
    return (new_factor, new_first, new_second, time_grad)


def solution(mesh):
    fine = Mesh(mesh.devices.reshape(2, 4, 8, 4, 2), AXES)
    rows = P(AXES, None)
    placed = (
        P(FEEDER_AXES, TM_AXES),
        P(FEEDER_AXES, TM_AXES),
        P(FEEDER_AXES, None),
        P(None, TM_AXES),
        P(),
        P(),
        rows,
        rows,
    )
    return jax.shard_map(
        per_device,
        mesh=fine,
        in_specs=placed,
        out_specs=(rows, rows, rows, P(FEEDER_AXES, TM_AXES)),
        check_vma=False,
    )
```

```python
import functools

import jax
import jax.numpy as jnp
from jax import lax
from jax.experimental import pallas as pl
from jax.experimental.pallas import tpu as pltpu
from jax.sharding import Mesh
from jax.sharding import PartitionSpec as P

LAGMAX = 1440
DATA_WEIGHT = 1.0 / 64.0
LAM_F = 0.1
LAM_X = 0.01
LAM_AR = 8.0
BETA_ONE = 0.9
BETA_TWO = 0.999
BIAS_FIRST = 1.0 - 0.9**8
BIAS_SECOND = 1.0 - 0.999**8
LEARNING_RATE = 0.05
ADAM_EPS = 1e-08

AXES = ("z_hi", "y", "z_lo", "x", "core")
FEEDER_AXES, TM_AXES = AXES[:2], AXES[2:]
PLANES, PLANE = 8, 8
TM = PLANES * PLANE
SHARE = 48
BAND = 8
SPAN = 512
TILES = SPAN // 128
MAIN_ROWS = PLANES * SHARE // 2
BAND_ROWS = BAND * TILES
ROWS = MAIN_ROWS + 2 * BAND_ROWS
HOPS = 3
CHUNKS = (HOPS + 1) * TILES


def gray(place):
    return place ^ (place >> 1)


def place_of(axes):
    place = 0
    for axis in axes:
        place = place * lax.axis_size(axis) + lax.axis_index(axis)
    return place


def main_kernel(
    observed, words, factor, time, keep, send, time_keep, time_send, total, *, steps, planes
):
    step = pl.program_id(0)
    factor_half = factor[...].astype(jnp.bfloat16)
    time_half = time[...].astype(jnp.bfloat16)
    predicted = lax.dot_general(
        factor_half, time_half, (((0,), (0,)), ((), ())), preferred_element_type=jnp.float32
    )
    word_count, span = words.shape[0], time.shape[1]
    spread = (
        lax.broadcasted_iota(jnp.int32, (word_count, span), 1) >> 3
        == lax.broadcasted_iota(jnp.int32, (word_count, span), 0)
    )
    power = 1.0 / jnp.left_shift(2, lax.broadcasted_iota(jnp.int32, (1, span), 1) & 7).astype(jnp.float32)
    spread = jnp.where(spread, power, 0.0).astype(jnp.bfloat16)
    wide = lax.dot_general(
        words[...].astype(jnp.float32).astype(jnp.bfloat16),
        spread,
        (((0,), (0,)), ((), ())),
        preferred_element_type=jnp.float32,
    )
    residual = jnp.where(
        wide - jnp.floor(wide) >= 0.5, predicted - observed[...].astype(jnp.float32), 0.0
    ).astype(jnp.bfloat16)
    rows = DATA_WEIGHT * lax.dot_general(
        residual, time_half, (((1,), (1,)), ((), ())), preferred_element_type=jnp.float32
    )
    half = SHARE // 2
    first = lax.axis_index("core") == 0
    for plane in range(planes):
        for x in range(PLANE // 2):
            pair = []
            for core in range(2):
                start = (plane * PLANE + 2 * x + core) * SHARE
                pair.append(
                    jnp.concatenate(
                        [rows[start : start + half], rows[start + half : start + SHARE]], axis=1
                    )
                )
            at = pl.ds(pl.multiple_of(x * MAIN_ROWS + (step * planes + plane) * half, 8), half)
            keep[at] = jnp.where(first, pair[0], pair[1])
            send[at] = jnp.where(first, pair[1], pair[0])
    term = jnp.dot(factor_half, residual, preferred_element_type=jnp.float32)

    @pl.when(step == 0)
    def _():
        total[...] = term
        own = time[pl.ds(pl.multiple_of(place_of(FEEDER_AXES) * BAND, BAND), BAND), :]
        for tile in range(TILES):
            at = PLANE // 2 * MAIN_ROWS + BAND * tile
            keep[at : at + BAND] = own[:, 128 * tile : 128 * tile + 128]
            send[at : at + BAND] = own[:, 128 * tile : 128 * tile + 128]

    @pl.when(step > 0)
    def _():
        total[...] = total[...] + term

    @pl.when(step == steps - 1)
    def _():
        z_hi, y_ring = lax.axis_index("z_hi"), gray(lax.axis_index("y"))
        for near in range(4):
            far = near ^ y_ring
            for z in range(2):
                band = (z ^ z_hi) * 4 + (far ^ (far >> 1))
                rows_out = DATA_WEIGHT * total[pl.ds(pl.multiple_of(band * BAND, BAND), BAND), :]
                if near & 1:
                    time_send[near >> 1, z] = rows_out
                else:
                    time_keep[near >> 1, z] = rows_out


def main_terms(observed, words, factor, time, steps=2):
    feeders, span = observed.shape
    ranks, block = factor.shape[0], feeders // steps
    half_rows = PLANE // 2 * MAIN_ROWS + BAND_ROWS
    return pl.pallas_call(
        functools.partial(main_kernel, steps=steps, planes=PLANES // steps),
        grid=(steps,),
        in_specs=[
            pl.BlockSpec((block, span), lambda s: (s, 0)),
            pl.BlockSpec((words.shape[0], block), lambda s: (0, s)),
            pl.BlockSpec((ranks, block), lambda s: (0, s)),
            pl.BlockSpec((ranks, span), lambda s: (0, 0)),
        ],
        out_specs=[
            pl.BlockSpec((half_rows, 128), lambda s: (0, 0)),
            pl.BlockSpec((half_rows, 128), lambda s: (0, 0)),
            pl.BlockSpec((2, 2, BAND, span), lambda s: (0, 0, 0, 0)),
            pl.BlockSpec((2, 2, BAND, span), lambda s: (0, 0, 0, 0)),
        ],
        scratch_shapes=[pltpu.VMEM((ranks, span), jnp.float32)],
        out_shape=[
            jax.ShapeDtypeStruct((half_rows, 128), jnp.float32),
            jax.ShapeDtypeStruct((half_rows, 128), jnp.float32),
            jax.ShapeDtypeStruct((2, 2, BAND, span), jnp.float32),
            jax.ShapeDtypeStruct((2, 2, BAND, span), jnp.float32),
        ],
        cost_estimate=pl.CostEstimate(flops=805306368, bytes_accessed=6_000_000, transcendentals=0),
        compiler_params=pltpu.CompilerParams(vmem_limit_bytes=24 << 20),
        name="main_terms",
    )(*(pltpu.with_memory_space_constraint(a, pltpu.HBM) for a in (observed, words, factor, time)))


def pair_kernel(keep, got, out):
    first = lax.axis_index("core") == 0
    tail = PLANE // 2 * MAIN_ROWS
    mine, other = keep[tail:], got[tail:]
    for x in range(PLANE // 2):
        at = slice(x * MAIN_ROWS, (x + 1) * MAIN_ROWS)
        out[x, :MAIN_ROWS] = keep[at] + got[at]
        out[x, MAIN_ROWS : MAIN_ROWS + BAND_ROWS] = jnp.where(first, mine, other)
        out[x, MAIN_ROWS + BAND_ROWS :] = jnp.where(first, other, mine)


def pair_terms(keep, got):
    in_vmem = pl.BlockSpec(memory_space=pltpu.VMEM)
    return pl.pallas_call(
        pair_kernel,
        in_specs=[in_vmem, in_vmem],
        out_specs=in_vmem,
        out_shape=jax.ShapeDtypeStruct((PLANE // 2, ROWS, 128), jnp.float32),
        cost_estimate=pl.CostEstimate(flops=100_000, bytes_accessed=1_400_000, transcendentals=0),
        compiler_params=pltpu.CompilerParams(vmem_limit_bytes=8 << 20),
        name="pair_terms",
    )(keep, got)


def split_kernel(got, planes, passed):
    total = got[0, :MAIN_ROWS]
    for x in range(1, PLANE // 2):
        total = total + got[x, :MAIN_ROWS]
    half = SHARE // 2
    for z in range(PLANES):
        planes[z] = total[half * z : half * z + half]
    late = place_of(AXES[3:]) < PLANE // 2
    for span in range(HOPS):
        ends = []
        for source in (PLANE - HOPS + span, span):
            at = MAIN_ROWS + BAND_ROWS * (source & 1)
            ends.append(got[source >> 1, at : at + BAND_ROWS])
        passed[span] = jnp.where(late, ends[0], ends[1])


def split_terms(got):
    in_vmem = pl.BlockSpec(memory_space=pltpu.VMEM)
    return pl.pallas_call(
        split_kernel,
        in_specs=[in_vmem],
        out_specs=[in_vmem, in_vmem],
        out_shape=[
            jax.ShapeDtypeStruct((PLANES, SHARE // 2, 128), jnp.float32),
            jax.ShapeDtypeStruct((HOPS, BAND_ROWS, 128), jnp.float32),
        ],
        cost_estimate=pl.CostEstimate(flops=100_000, bytes_accessed=700_000, transcendentals=0),
        compiler_params=pltpu.CompilerParams(vmem_limit_bytes=8 << 20),
        name="split_terms",
    )(got)


def shifted_tiles(start, count, read):
    first, lane = start >> 7, start & 127
    back = (128 - lane) & 127
    rolled = [pltpu.roll(read(first + i), back, 1) for i in range(count + 1)]
    inside = lax.broadcasted_iota(jnp.int32, (BAND, 128), 1) < 128 - lane
    return [jnp.where(inside, rolled[i], rolled[i + 1]) for i in range(count)]


def ar_kernel(lags, weights, plane, beside, home, out, spans, errors, weight_rows):
    edge = HOPS * TILES
    for span in range(HOPS):
        for tile in range(TILES):
            value = beside[span, BAND * tile : BAND * tile + BAND]
            spans[span * TILES + tile] = value
            spans[edge + PLANE * TILES + span * TILES + tile] = value
    for span in range(PLANE):
        for tile in range(TILES):
            spans[edge + span * TILES + tile] = plane[span, BAND * tile : BAND * tile + BAND]
    weight_rows[...] = weights[...].T
    mine = weight_rows[pl.ds(pl.multiple_of(place_of(FEEDER_AXES) * BAND, BAND), BAND), :]
    own_tile = edge + place_of(AXES[3:]) * TILES
    own_column = own_tile * 128
    count = lags.shape[0]
    gains = [jnp.broadcast_to(mine[:, k : k + 1], (BAND, 128)) for k in range(count)]
    lane = lax.broadcasted_iota(jnp.int32, (BAND, 128), 1)
    first = place_of(TM_AXES) * SPAN
    for begin, end in ((0, TILES + 1), (LAGMAX >> 7, CHUNKS)):
        parts = [jnp.zeros((BAND, 128), jnp.float32) for _ in range(begin, end)]
        for k in range(count):
            start = own_column + 128 * begin - lags[k]
            moved = shifted_tiles(start, end - begin, lambda i: spans[i])
            parts = [part + gains[k] * tile for part, tile in zip(parts, moved)]
        for chunk, part in zip(range(begin, end), parts):
            column = first + 128 * chunk + lane
            inside = (column >= LAGMAX) & (column < TM * SPAN)
            errors[chunk] = jnp.where(inside, spans[own_tile + chunk] - part, 0.0)
    carried = [jnp.zeros((BAND, 128), jnp.float32) for _ in range(TILES)]
    for k in range(count):
        moved = shifted_tiles(lags[k], TILES, lambda i: errors[i])
        carried = [part + gains[k] * tile for part, tile in zip(carried, moved)]
    for tile in range(TILES):
        at = slice(128 * tile, 128 * tile + 128)
        out[:, at] = (
            home[:, at]
            + LAM_AR * (errors[tile] - carried[tile])
            + LAM_X * spans[own_tile + tile]
        )


def ar_terms(lags, weights, plane, beside, home):
    in_vmem = pl.BlockSpec(memory_space=pltpu.VMEM)
    in_smem = pl.BlockSpec(memory_space=pltpu.SMEM)
    tiles = (2 * HOPS + PLANE) * TILES
    return pl.pallas_call(
        ar_kernel,
        in_specs=[in_smem] + [in_vmem] * 4,
        out_specs=in_vmem,
        out_shape=jax.ShapeDtypeStruct((BAND, SPAN), jnp.float32),
        scratch_shapes=[
            pltpu.VMEM((tiles + 1, BAND, 128), jnp.float32),
            pltpu.VMEM((CHUNKS, BAND, 128), jnp.float32),
            pltpu.VMEM(weights.shape[::-1], jnp.float32),
        ],
        cost_estimate=pl.CostEstimate(flops=2_000_000, bytes_accessed=400_000, transcendentals=0),
        compiler_params=pltpu.CompilerParams(vmem_limit_bytes=8 << 20),
        name="ar_terms",
    )(lags, weights, plane, beside, home)


def per_device(
    observed, mask_words, feeder_factor, time_factor, ar_weight, lags, moment_first, moment_second
):
    ranks = time_factor.shape[0]
    tm_place = lax.axis_index(TM_AXES)

    keep, send, bands, sent_bands = main_terms(observed, mask_words.T, feeder_factor.T, time_factor)
    got = lax.ppermute(send, "core", [(0, 1), (1, 0)])
    own_factor = lax.dynamic_slice_in_dim(feeder_factor, tm_place * SHARE, SHARE, 0)
    bands = bands + lax.ppermute(sent_bands, "y", [(0, 1), (1, 0), (2, 3), (3, 2)])
    pair = pair_terms(keep, got)
    bands = bands[0] + lax.ppermute(bands[1], "y", [(0, 3), (3, 0), (1, 2), (2, 1)])
    got = lax.all_to_all(pair, "x", 0, 0, tiled=True)
    away = lax.ppermute(bands[1], "z_hi", [(0, 1), (1, 0)])

    planes, passed = split_terms(got)
    plane = got[:, MAIN_ROWS:].reshape(PLANE, BAND_ROWS, 128)
    pairs = [(t, t + PLANE) for t in range(TM - PLANE) if t % PLANE < PLANE // 2]
    pairs += [(t, t - PLANE) for t in range(PLANE, TM) if t % PLANE >= PLANE // 2]
    beside = lax.ppermute(passed, TM_AXES, pairs)
    share = lax.all_to_all(planes, "z_lo", 0, 0, tiled=True)
    share = share.sum(0)
    half_grad = ar_terms(lags, ar_weight, plane, beside, bands[0])
    time_grad = half_grad + away

    grad_share = jnp.concatenate([share[:, :ranks], share[:, ranks:]], axis=0)
    factor_grad = grad_share + LAM_F * own_factor
    new_first = BETA_ONE * moment_first + (1.0 - BETA_ONE) * factor_grad
    new_second = BETA_TWO * moment_second + (1.0 - BETA_TWO) * factor_grad * factor_grad
    update = (
        LEARNING_RATE * (new_first / BIAS_FIRST) / (jnp.sqrt(new_second / BIAS_SECOND) + ADAM_EPS)
    )
    new_factor = own_factor - update
    return (new_factor, new_first, new_second, time_grad)


def solution(mesh):
    fine = Mesh(mesh.devices.reshape(2, 4, 8, 4, 2), AXES)
    rows = P(AXES, None)
    placed = (
        P(FEEDER_AXES, TM_AXES),
        P(FEEDER_AXES, TM_AXES),
        P(FEEDER_AXES, None),
        P(None, TM_AXES),
        P(),
        P(),
        rows,
        rows,
    )
    return jax.shard_map(
        per_device,
        mesh=fine,
        in_specs=placed,
        out_specs=(rows, rows, rows, P(FEEDER_AXES, TM_AXES)),
        check_vma=False,
    )
```
